128 devices in a mesh: row: 8 (over x, y_hi), col: 16 (over y_lo, z, core).
Axes of the slice: x: 4, y: 4 (y_hi: 2, y_lo: 2; y = y_hi * 2 + y_lo), z: 4, core: 2. Of those that a mesh axis runs over, the one named last changes fastest.
Arguments:
- amplitude: float32 [800, 20480], P('row', 'col'), may hold values from -6 to 6
- ladder_coupling: float32 [20480, 20480], P('row', 'col'), may hold values from -0.0390625 to 0.0390625
- crossed_coupling: float32 [8, 1280, 1280], P('row'), may hold values from -0.15625 to 0.15625
- channel_slot: int32 [8], replicated, may hold values from 0 to 7, each once
- channel_of: int32 [16, 1024, 1], P('col', 'row'), may hold values from 0 to 7; in each aligned block of 128 rows (0 to 127, 128 to 255, ..., all dimensions but the last counted through in order) at most 40 rows name the same one
- source_row: int32 [16, 1024], P('col', 'row'), may hold values from 0 to 799
- target_row: int32 [16, 1024], P('col', 'row'), may hold values from 0 to 1599
- recoupling: float32 [16, 1024], P('col', 'row'), may hold values from -1 to 1
- driving: float32 [800, 20480], P('col', 'row'), may hold values from -6 to 6
- denominator: float32 [800, 20480], P('col', 'row'), may hold values from 1 to 10
Outputs:
- updated: float32 [800, 20480], P('col', 'row')
The draws below stay inside these ranges and needn't reach their ends.
Inputs may be any that keep to these rules, and one draw needn't show every extreme that they name: Among the 128 segments of one device (aligned blocks of channel_of's rows), no channel is named more than 40 times; some channel is named exactly 40 times in some device's segments. `channel_slot`: each slot once.
All inputs are finite; a program needn't handle non-finite values.
Results may differ from the reference program's by a relative error of at most 0.0003.
Values sent between devices are 32-bit elements; how exact they have to be, the bound alone decides.
A program may use at most 128 MiB of HBM per device.

```python
import math
import jax
import jax.numpy as jnp
import numpy as np
from jax import lax

H = 800
P_SIZE = 20480
W = 1280
ITEMS = 128
NCH = 8
CAP = 40
ITEMS_ALL = 1024
SEG_IN = 1
SEG_OUT = 2
N_ROW = 8
N_COL = 16


def set_ends(values, own_key, least, high):
    longest = values.shape.index(max(values.shape))
    spots = []
    for shift in (0, 1):
        where = [jax.random.randint(jax.random.fold_in(own_key, axis), (), 0, length) for axis, length in enumerate(values.shape)]
        where[longest] = (where[longest] + shift) % values.shape[longest]
        spots.append(tuple(where))
    return values.at[spots[0]].set(least).at[spots[1]].set(high)


def block_levels(rng, extent, shards, least, top_value):
    gain = 1.0
    for dim, blocks in shards:
        heights = jax.random.uniform(jax.random.fold_in(jax.random.fold_in(rng, 6), dim), (blocks,), jnp.float32, least / len(shards), top_value / len(shards))
        gain = gain * jnp.repeat(jnp.exp(heights), extent[dim] // blocks).reshape((-1,) + (1,) * (len(extent) - 1 - dim))
    return gain


def shared_out(stream_key, own, number, rows, number_of, top, most, skew):
    sequence = jax.random.permutation(stream_key, number_of)
    crowded, common = load_shares(number_of, rows * top, most, skew, True), load_shares(number_of, rows * top, most, skew, False)
    places = jnp.arange(number_of)

    def named(tallies, turn):
        used = int((tallies > 0).sum())
        fixed = max(1, used // 4)
        shifted = fixed + (places - fixed + turn * (used - fixed)) % max(1, number_of - fixed)
        return jnp.zeros((number_of,), jnp.int32).at[sequence[jnp.where(places < fixed, places, shifted)]].set(jnp.asarray(tallies, jnp.int32))

    tallies = jnp.where(number % 4 == 0, named(crowded, number // 4), named(common, number - number // 4 - 1))
    mixed = jax.random.permutation(jax.random.fold_in(own, 3), number_of)
    donor, sink = mixed[0:number_of // 2 * 2:2], mixed[1:number_of // 2 * 2:2]
    slack = jnp.minimum(tallies[donor] - 1, most - tallies[sink]) // 2
    slack = jnp.where((donor == sequence[0]) | (sink == sequence[0]) | (tallies[sink] == 0), 0, jnp.maximum(slack, 0))
    shifted = jax.random.randint(jax.random.fold_in(own, 4), (number_of // 2,), 0, 1 << 20) % (slack + 1)
    tallies = tallies.at[donor].add(-shifted).at[sink].add(shifted)
    members = jnp.searchsorted(jnp.cumsum(tallies), jnp.arange(rows * top), side="right").astype(jnp.int32)
    grid = members.reshape(top, rows).T
    grid = grid[jax.random.permutation(jax.random.fold_in(own, 1), rows)]
    turn = jax.random.randint(jax.random.fold_in(own, 2), (rows, 1), 0, top)
    return jnp.take_along_axis(grid, (jnp.arange(top)[None, :] + turn) % top, axis=1)


def load_shares(count, total, most, lean, full):
    loads = [(1 << 20) // math.isqrt(rank ** lean) + 1 for rank in range(1, count + 1)]
    largest = most if full else min(most, max(-(-total // count), total * loads[0] // sum(loads)))
    least = 1 if total - largest >= count - 1 else 0
    holding, spare = [largest] + [least] * (count - 1), total - largest - least * (count - 1)
    while spare > 0:
        movable = [i for i in range(1, count) if holding[i] < largest] or [i for i in range(1, count) if holding[i] < most]
        mass, left = sum([loads[i] for i in movable]), spare
        for i in movable:
            more = min(most - holding[i], max(1, left * loads[i] // mass), spare)
            holding[i] = holding[i] + more
            spare = spare - more
    return np.array(holding)


def scatter_about(rng, dims, width, reach, split=(), kind=jnp.bfloat16):
    drawn = jax.random.normal(rng, dims, jnp.float32) * width
    if len(split) > 0:
        drawn = block_levels(rng, dims, split, -0.22, 0.18) * drawn
    return jnp.clip(drawn, min=-reach, max=reach).astype(kind)


def setup_inputs(seed: int = 0) -> dict:
    key_of = jax.random.split(jax.random.key(seed), 11)
    amplitude = scatter_about(key_of[0], (H, P_SIZE), 1.0, 6.0, ((0, 8), (1, 16)), jnp.float32)
    ladder_coupling = scatter_about(key_of[1], (P_SIZE, P_SIZE), P_SIZE ** -0.5, 0.0390625, ((0, 8), (1, 16)), jnp.float32)
    crossed_coupling = scatter_about(key_of[2], (NCH, W, W), W ** -0.5, 0.15625, ((0, 8),), jnp.float32)
    channel_slot = jax.random.permutation(key_of[3], NCH).astype(jnp.int32)
    channel_of_keys = jax.random.split(jax.random.fold_in(key_of[4], 1), N_COL * ITEMS_ALL // ITEMS)
    channel_of_turns = jax.random.permutation(jax.random.fold_in(key_of[4], 3), N_COL * ITEMS_ALL // ITEMS)
    channel_of = jax.vmap(lambda own, number: shared_out(jax.random.fold_in(key_of[4], 2), own, number, ITEMS, NCH, 1, CAP, 2))(channel_of_keys, channel_of_turns).reshape((N_COL, ITEMS_ALL, 1))
    source_row = set_ends(jax.random.randint(key_of[5], (N_COL, ITEMS_ALL), 0, H * SEG_IN), jax.random.fold_in(key_of[5], 1), 0, (H * SEG_IN) - 1).astype(jnp.int32)
    target_row = set_ends(jax.random.randint(key_of[6], (N_COL, ITEMS_ALL), 0, H * SEG_OUT), jax.random.fold_in(key_of[6], 1), 0, (H * SEG_OUT) - 1).astype(jnp.int32)
    recoupling = jnp.clip(jax.random.uniform(key_of[7], (N_COL, ITEMS_ALL), jnp.float32, -1.0, 1.0) * block_levels(key_of[7], (N_COL, ITEMS_ALL), ((0, 16), (1, 8)), -0.4, 0.0), -1.0, 1.0)
    driving = scatter_about(key_of[8], (H, P_SIZE), 1.0, 6.0, ((0, 16), (1, 8)), jnp.float32)
    denominator = jnp.clip(jnp.exp(math.log(10.0) - 2.3025851 * jax.random.uniform(key_of[9], (H, P_SIZE), jnp.float32) ** block_levels(key_of[9], (H, P_SIZE), ((0, 16), (1, 8)), -0.2, 0.2)), 1.0, 10.0)
    return {"amplitude": amplitude, "ladder_coupling": ladder_coupling, "crossed_coupling": crossed_coupling, "channel_slot": channel_slot, "channel_of": channel_of, "source_row": source_row, "target_row": target_row, "recoupling": recoupling, "driving": driving, "denominator": denominator}


def reference(amplitude, ladder_coupling, crossed_coupling, channel_slot, channel_of, source_row, target_row, recoupling, driving, denominator):
    highest = lax.Precision.HIGHEST
    ladder = lax.dot_general(amplitude, ladder_coupling, (((1,), (1,)), ((), ())), precision=highest, preferred_element_type=jnp.float32)
    blocks = amplitude.reshape(H, N_COL, SEG_IN, W).transpose(1, 0, 2, 3).reshape(N_COL, H * SEG_IN, W)
    picked = jax.vmap(lambda table_rows, chosen: table_rows[chosen])(blocks, source_row)
    picked = picked * recoupling[:, :, None]
    owners = channel_slot[channel_of[:, :, 0]]

    def add_channel(accumulated, slot_id):
        matrix = lax.dynamic_index_in_dim(crossed_coupling, slot_id, 0, keepdims=False)
        product = jnp.einsum("cnw,wv->cnv", picked, matrix, precision=highest, preferred_element_type=jnp.float32)
        return accumulated + jnp.where((owners == slot_id)[:, :, None], product, jnp.float32(0.0)), None

    crossed, _ = lax.scan(add_channel, jnp.zeros(picked.shape, jnp.float32), jnp.arange(NCH, dtype=jnp.int32))
    hole_index = target_row // SEG_OUT
    segment_index = target_row % SEG_OUT
    block_index = jnp.broadcast_to((jnp.arange(ITEMS_ALL, dtype=jnp.int32) // ITEMS)[None, :], target_row.shape)
    particle_hole = jnp.zeros((H, N_ROW, SEG_OUT, W), jnp.float32).at[hole_index, block_index, segment_index].add(crossed)
    particle_hole = particle_hole.reshape(H, P_SIZE)
    return (driving + ladder + particle_hole) / denominator
```

```python
import jax
import jax.numpy as jnp
from jax import lax
from jax.experimental import pallas as pl
from jax.experimental.pallas import tpu as pltpu
from jax.sharding import PartitionSpec as P

CAP = 40
NROW = 8
PAD = 104
CHUNK = 256
MESH = pl.DeviceIdType.MESH
F32 = jnp.float32
BF16 = jnp.bfloat16
OFFSETS = [(dx, dy) for dx in (1, 3, 2, 0) for dy in (0, 1) if (dx, dy) != (0, 0)]


def split(value):
    high = value.astype(BF16)
    return high, (value - high.astype(F32)).astype(BF16)


def dot(a, b):
    return lax.dot_general(a, b, (((1,), (0,)), ((), ())), preferred_element_type=F32)


def dot_t(a, b):
    return lax.dot_general(a, b, (((1,), (1,)), ((), ())), preferred_element_type=F32)


def kernel(
    meta, tgt, amp, lad, xm, out,
    own, gath, ahi, alo, stage, chi, clo, xstage, xhi, xlo, mrecv, colb, colc, pacc, phi, plo, onehot,
    cross, back, sib, mine, crecv, zrecv, yrecv, esend, erecv,
    lsem, stsem, gs, gr, ms, mr, ts, tr, cs, cr, zs, zr, ys, yr, es, er,
):
    rows, width = amp.shape
    chunks = width // CHUNK
    half = width // 2
    r, c = lax.axis_index("row"), lax.axis_index("col")
    x, yh = r // 2, r % 2
    yl, z, core = c // 8, (c // 2) % 4, c % 2
    xp, xm1, x2 = (x + 1) % 4, (x + 3) % 4, (x + 2) % 4
    zp, zm, z2 = (z + 1) % 4, (z + 3) % 4, (z + 2) % 4

    def row_dev(i):
        dx, dy = OFFSETS[i]
        return ((x + dx) % 4) * 2 + (yh + dy) % 2

    def row_src(i):
        dx, dy = OFFSETS[i]
        return ((x + 4 - dx) % 4) * 2 + (yh + dy) % 2

    sibling = (r, yl * 8 + z * 2 + (1 - core))
    above = (r, yl * 8 + zp * 2 + core)
    below = (r, yl * 8 + zm * 2 + core)
    beside = (r, (1 - yl) * 8 + z * 2 + core)
    right, left, across = (xp * 2 + yh, c), (xm1 * 2 + yh, c), (x * 2 + 1 - yh, c)

    def remote(src, dst, send, recv, device):
        return pltpu.make_async_remote_copy(
            src_ref=src, dst_ref=dst, send_sem=send, recv_sem=recv, device_id=device, device_id_type=MESH
        )

    def load_ladder(p):
        return pltpu.make_async_copy(
            lad.at[pl.ds(pl.multiple_of(p * CHUNK, CHUNK), CHUNK), :], stage.at[p % 2], stsem.at[p % 2]
        )

    def load_cross(p):
        return pltpu.make_async_copy(
            xm.at[0, :, pl.ds(pl.multiple_of(p * CHUNK, CHUNK), CHUNK)], xstage.at[p % 2], stsem.at[2 + p % 2]
        )

    load_own = pltpu.make_async_copy(amp, own, lsem)
    load_own.start()
    load_ladder(0).start()
    load_cross(0).start()

    barrier = pltpu.get_barrier_semaphore()
    partners = [(row_dev(i), c) for i in range(7)] + [sibling, above, below, beside]
    for device in partners:
        pl.semaphore_signal(barrier, inc=1, device_id=device, device_id_type=MESH)
    load_own.wait()
    gath[r, 0:rows, :] = own[...]
    gath[r, rows:PAD, :] = jnp.zeros((PAD - rows, width), F32)
    pl.semaphore_wait(barrier, len(partners))

    def hop(i, shard, device, columns=None):
        ref = gath.at[shard] if columns is None else gath.at[shard, :, pl.ds(columns, half)]
        return remote(ref, ref, gs.at[i], gr.at[i], device)

    g1, g2, g3 = hop(0, r, right), hop(1, r, left), hop(2, r, across)
    g1.start()
    g2.start()
    g3.start()
    mcopies = []
    for i in range(7):
        copy = remote(meta.at[row_dev(i)], mrecv.at[r], ms.at[i], mr.at[i], (row_dev(i), c))
        copy.start()
        mcopies.append(copy)
    mrecv[r] = meta[r]

    @pl.loop(0, 2 * chunks)
    def _(p):
        load_ladder(p).wait()

        @pl.when(p + 1 < 2 * chunks)
        def _():
            load_ladder(p + 1).start()

        high, low = split(stage[p % 2])
        chi[p] = high
        clo[p] = low

    n_left, n_right, n_across = xm1 * 2 + yh, xp * 2 + yh, x * 2 + 1 - yh
    hop(0, n_left, right).wait_recv()
    g4 = hop(3, n_left, right, 0)
    g4.start()
    hop(1, n_right, left).wait_recv()
    g5 = hop(4, n_right, left, half)
    g5.start()
    hop(2, n_across, across).wait_recv()
    g6, g7 = hop(5, n_across, right), hop(6, n_across, left)
    g6.start()
    g7.start()

    @pl.loop(0, chunks)
    def _(p):
        load_cross(p).wait()

        @pl.when(p + 1 < chunks)
        def _():
            load_cross(p + 1).start()

        high, low = split(xstage[p % 2])
        xhi[p] = high
        xlo[p] = low

    slots = NROW * CAP
    group = 2 * PAD
    for s in range(2):
        for g in range(4):
            place = (lax.broadcasted_iota(jnp.int32, (group, slots), 0) + g * group).astype(F32)
            hit = jnp.where(place == tgt[s : s + 1, 0:slots], 1.0, 0.0)
            onehot[s, g] = hit.astype(BF16)

    for i in range(7):
        remote(meta.at[r], mrecv.at[row_src(i)], ms.at[i], mr.at[i], (row_src(i), c)).wait_recv()
    diagonal = lax.broadcasted_iota(jnp.int32, (CAP, 128), 0) == lax.broadcasted_iota(jnp.int32, (CAP, 128), 1)
    for s in range(NROW):
        for row, target in ((0, colb), (1, colc)):
            column = jnp.sum(jnp.where(diagonal, mrecv[s, row : row + 1, :], 0.0), axis=1, keepdims=True)
            target[s * CAP : (s + 1) * CAP, :] = jnp.broadcast_to(column, (CAP, 128))

    def take(g, first):
        high, low = split(gath[pl.ds(g * 2, 2)].reshape(group, width))
        ahi[g] = high
        alo[g] = low
        place = (lax.broadcasted_iota(jnp.int32, (slots, group), 1) + g * group).astype(F32)
        chosen = jnp.where(place == colb[:, 0:1], 1.0, 0.0).astype(BF16)
        for n in range(chunks):
            columns = slice(n * CHUNK, (n + 1) * CHUNK)
            part = dot(chosen, ahi[g, :, columns]) + dot(chosen, alo[g, :, columns])
            if first:
                pacc[:, columns] = part
            else:
                pacc[:, columns] += part

    take(x, True)
    n_far = x2 * 2 + yh
    hop(3, n_far, right, 0).wait_recv()
    hop(4, n_far, left, half).wait_recv()
    g8 = hop(7, n_far, across)
    g8.start()
    hop(5, xm1 * 2 + 1 - yh, right).wait_recv()
    take(xm1, False)
    hop(6, xp * 2 + 1 - yh, left).wait_recv()
    take(xp, False)
    hop(7, x2 * 2 + 1 - yh, across).wait_recv()
    take(x2, False)
    for n in range(chunks):
        columns = slice(n * CHUNK, (n + 1) * CHUNK)
        high, low = split(pacc[:, columns] * colc[:, 0:1])
        phi[:, columns] = high
        plo[:, columns] = low

    def returned(k, i, source):
        return remote(cross.at[k, source], back.at[k, r], ts.at[k, i], tr.at[k, i], (source, c))

    def product(k):
        value = dot(phi[...], xhi[k]) + dot(plo[...], xhi[k]) + dot(phi[...], xlo[k])
        cross[k] = value.reshape(NROW, CAP, CHUNK)
        for i in range(7):
            returned(k, i, row_dev(i)).start()
        back[k, r] = cross[k, r]

    def ladder(s, k, target):
        p = s * chunks + k

        @pl.loop(0, 4)
        def _(g):
            value = dot_t(ahi[g], chi[p]) + dot_t(alo[g], chi[p]) + dot_t(ahi[g], clo[p])
            target[pl.ds(g * 2, 2)] = value.reshape(2, PAD, CHUNK)

    def scatter(s, k, target):
        high, low = split(back[k].reshape(slots, CHUNK))

        @pl.loop(0, 4)
        def _(g):
            value = dot(onehot[s, g], high) + dot(onehot[s, g], low)
            target[pl.ds(g * 2, 2)] += value.reshape(2, PAD, CHUNK)

    def to_sibling(k):
        return remote(sib.at[k % 2], crecv.at[k], cs.at[k], cr.at[k], sibling)

    def unit(k, depth, side):
        return mine.at[k, side * 4 + depth]

    def around(k, i):
        sources = [
            (unit(k, z2, 0), above),
            (unit(k, z2, 1), below),
            (unit(k, zp, 1), above),
            (unit(k, zm, 0), below),
            (unit(k, zp, 0), above),
            (unit(k, zm, 1), below),
        ]
        return remote(sources[i][0], zrecv.at[k, i], zs.at[k, i], zr.at[k, i], sources[i][1])

    def aside(k):
        return remote(unit(k, z, 1 - yl), yrecv.at[k], ys.at[k], yr.at[k], beside)

    def exchange(k):
        return remote(esend.at[k], erecv.at[k], es.at[k], er.at[k], sibling)

    product(0)
    block = rows // 2

    @pl.loop(0, chunks + 4)
    def _(t):
        @pl.when(t < chunks)
        def _():
            @pl.when(t + 1 < chunks)
            def _():
                product(t + 1)

            @pl.when(t >= 2)
            def _():
                to_sibling(t - 2).wait_send()

            ladder(1 - core, t, sib.at[t % 2])
            for i in range(7):
                remote(
                    cross.at[t, r], back.at[t, row_src(i)], ts.at[t, i], tr.at[t, i], (row_src(i), c)
                ).wait_recv()
            scatter(1 - core, t, sib.at[t % 2])
            to_sibling(t).start()
            ladder(core, t, mine.at[t])
            scatter(core, t, mine.at[t])
            to_sibling(t).wait_recv()
            mine[t] += crecv[t]
            for i in range(4):
                around(t, i).start()

        @pl.when((t >= 1) & (t < chunks + 1))
        def _():
            k = t - 1
            around(k, 0).wait_recv()
            mine[k, zp] += zrecv[k, 0]
            around(k, 4).start()
            around(k, 1).wait_recv()
            mine[k, 4 + zm] += zrecv[k, 1]
            around(k, 5).start()

        @pl.when((t >= 2) & (t < chunks + 2))
        def _():
            k = t - 2
            for i in range(2, 6):
                around(k, i).wait_recv()
            mine[k, z] += zrecv[k, 3] + zrecv[k, 4]
            mine[k, 4 + z] += zrecv[k, 2] + zrecv[k, 5]
            aside(k).start()

        @pl.when((t >= 3) & (t < chunks + 3))
        def _():
            k = t - 3
            aside(k).wait_recv()
            mine[k, yl * 4 + z] += yrecv[k]
            low = mine[k, yl * 4 + z, 0:block, :]
            high = mine[k, yl * 4 + z, block:rows, :]
            esend[k] = jnp.where(core == 0, high, low)
            exchange(k).start()
            out[:, pl.ds(pl.multiple_of(core * width + k * CHUNK, CHUNK), CHUNK)] = jnp.where(core == 0, low, high)

        @pl.when(t >= 4)
        def _():
            k = t - 4
            exchange(k).wait_recv()
            out[:, pl.ds(pl.multiple_of((1 - core) * width + k * CHUNK, CHUNK), CHUNK)] = erecv[k]

    for copy in [g1, g2, g3, g4, g5, g6, g7, g8] + mcopies:
        copy.wait_send()

    @pl.loop(0, chunks)
    def _(k):
        for i in range(7):
            returned(k, i, row_dev(i)).wait_send()
        for i in range(6):
            around(k, i).wait_send()
        aside(k).wait_send()
        exchange(k).wait_send()

    to_sibling(chunks - 2).wait_send()
    to_sibling(chunks - 1).wait_send()


def tables(channel_slot, channel_of, source_row, target_row, recoupling, shard):
    names = jnp.arange(NROW, dtype=jnp.int32)
    named = channel_of[0] == names[None, :]
    owners = jnp.sum(jnp.where(named, channel_slot[None, :], 0), axis=1)
    marks = (owners[:, None] == names[None, :]).astype(jnp.int32)
    before = jnp.cumsum(marks, axis=0) - marks
    slot = owners * CAP + jnp.sum(before * marks, axis=1)
    match = slot[None, :] == jnp.arange(NROW * CAP, dtype=jnp.int32)[:, None]
    pad = PAD - shard
    source = source_row[0] + pad * (source_row[0] // shard)
    hole = target_row[0] // 2
    hole = hole + pad * (hole // shard)
    odd = target_row[0] % 2

    def place(value, where):
        return (jnp.sum(jnp.where(where, value[None, :] + 1, 0), axis=1) - 1).astype(F32)

    chosen = place(source, match)
    scale = jnp.sum(jnp.where(match, recoupling[0][None, :], 0.0), axis=1)
    even_target = place(hole, match & (odd == 0)[None, :])
    odd_target = place(hole, match & (odd == 1)[None, :])
    meta = jnp.stack([chosen.reshape(NROW, CAP), scale.reshape(NROW, CAP)], axis=1)
    meta = jnp.pad(meta, ((0, 0), (0, 6), (0, 128 - CAP)))
    return meta, jnp.stack([even_target, odd_target])


def on_device(
    amplitude,
    ladder_coupling,
    crossed_coupling,
    channel_slot,
    channel_of,
    source_row,
    target_row,
    recoupling,
    driving,
    denominator,
):
    rows, width = amplitude.shape
    chunks = width // CHUNK
    slots = NROW * CAP
    group = 2 * PAD
    meta, tgt = tables(channel_slot, channel_of, source_row, target_row, recoupling, rows)
    dma = pltpu.SemaphoreType.DMA
    vmem = pltpu.VMEM
    summed = pl.pallas_call(
        kernel,
        out_shape=jax.ShapeDtypeStruct((rows // 2, 2 * width), F32),
        in_specs=[pl.BlockSpec(memory_space=pltpu.VMEM)] * 2 + [pl.BlockSpec(memory_space=pl.ANY)] * 3,
        out_specs=pl.BlockSpec(memory_space=pltpu.VMEM),
        scratch_shapes=[
            vmem((rows, width), F32),
            vmem((NROW, PAD, width), F32),
            vmem((4, group, width), BF16),
            vmem((4, group, width), BF16),
            vmem((2, CHUNK, width), F32),
            vmem((2 * chunks, CHUNK, width), BF16),
            vmem((2 * chunks, CHUNK, width), BF16),
            vmem((2, width, CHUNK), F32),
            vmem((chunks, width, CHUNK), BF16),
            vmem((chunks, width, CHUNK), BF16),
            vmem((NROW, 8, 128), F32),
            vmem((slots, 128), F32),
            vmem((slots, 128), F32),
            vmem((slots, width), F32),
            vmem((slots, width), BF16),
            vmem((slots, width), BF16),
            vmem((2, 4, group, slots), BF16),
            vmem((chunks, NROW, CAP, CHUNK), F32),
            vmem((chunks, NROW, CAP, CHUNK), F32),
            vmem((2, NROW, PAD, CHUNK), F32),
            vmem((chunks, NROW, PAD, CHUNK), F32),
            vmem((chunks, NROW, PAD, CHUNK), F32),
            vmem((chunks, 6, PAD, CHUNK), F32),
            vmem((chunks, PAD, CHUNK), F32),
            vmem((chunks, rows // 2, CHUNK), F32),
            vmem((chunks, rows // 2, CHUNK), F32),
            dma,
            dma((4,)),
            dma((8,)),
            dma((8,)),
            dma((7,)),
            dma((7,)),
            dma((chunks, 7)),
            dma((chunks, 7)),
            dma((chunks,)),
            dma((chunks,)),
            dma((chunks, 6)),
            dma((chunks, 6)),
            dma((chunks,)),
            dma((chunks,)),
            dma((chunks,)),
            dma((chunks,)),
        ],
        compiler_params=pltpu.CompilerParams(
            collective_id=0, has_side_effects=True, vmem_limit_bytes=63 * 1024 * 1024
        ),
        cost_estimate=pl.CostEstimate(flops=24_000_000_000, bytes_accessed=22_000_000, transcendentals=0),
    )(meta, tgt, amplitude, ladder_coupling, crossed_coupling)
    return (driving + summed) / denominator


def solution(mesh):
    in_specs = (
        P("row", "col"),
        P("row", "col"),
        P("row", None, None),
        P(),
        P("col", "row", None),
        P("col", "row"),
        P("col", "row"),
        P("col", "row"),
        P("col", "row"),
        P("col", "row"),
    )
    out_specs = P("col", "row")
    return jax.shard_map(
        on_device, mesh=mesh, in_specs=in_specs, out_specs=out_specs, check_vma=False
    )
```

```python
import jax
import jax.numpy as jnp
from jax import lax
from jax.experimental import pallas as pl
from jax.experimental.pallas import tpu as pltpu
from jax.sharding import PartitionSpec as P

CAP = 40
NROW = 8
PAD = 104
CHUNK = 256
MESH = pl.DeviceIdType.MESH
F32 = jnp.float32
BF16 = jnp.bfloat16
OFFSETS = [(dx, dy) for dx in (1, 3, 2, 0) for dy in (0, 1) if (dx, dy) != (0, 0)]


def split(value):
    high = value.astype(BF16)
    return high, (value - high.astype(F32)).astype(BF16)


def dot(a, b):
    return lax.dot_general(a, b, (((1,), (0,)), ((), ())), preferred_element_type=F32)


def dot_t(a, b):
    return lax.dot_general(a, b, (((1,), (1,)), ((), ())), preferred_element_type=F32)


def kernel(
    meta, tgt, amp, lad, xm, out,
    own, gath, ahi, alo, stage, chi, clo, xstage, xhi, xlo, mrecv, colb, colc, pacc, phi, plo, onehot,
    cross, back, sib, mine, crecv, zrecv, hrecv, yrecv, esend, erecv,
    lsem, stsem, gs, gr, ms, mr, ts, tr, cs, cr, zs, zr, ys, yr, es, er,
):
    rows, width = amp.shape
    chunks = width // CHUNK
    half = width // 2
    r, c = lax.axis_index("row"), lax.axis_index("col")
    x, yh = r // 2, r % 2
    yl, z, core = c // 8, (c // 2) % 4, c % 2
    xp, xm1, x2 = (x + 1) % 4, (x + 3) % 4, (x + 2) % 4
    zp, zm, z2 = (z + 1) % 4, (z + 3) % 4, (z + 2) % 4

    def row_dev(i):
        dx, dy = OFFSETS[i]
        return ((x + dx) % 4) * 2 + (yh + dy) % 2

    def row_src(i):
        dx, dy = OFFSETS[i]
        return ((x + 4 - dx) % 4) * 2 + (yh + dy) % 2

    sibling = (r, yl * 8 + z * 2 + (1 - core))
    above = (r, yl * 8 + zp * 2 + core)
    below = (r, yl * 8 + zm * 2 + core)
    beside = (r, (1 - yl) * 8 + z * 2 + core)
    right, left, across = (xp * 2 + yh, c), (xm1 * 2 + yh, c), (x * 2 + 1 - yh, c)

    def remote(src, dst, send, recv, device):
        return pltpu.make_async_remote_copy(
            src_ref=src, dst_ref=dst, send_sem=send, recv_sem=recv, device_id=device, device_id_type=MESH
        )

    def load_ladder(p):
        return pltpu.make_async_copy(
            lad.at[pl.ds(pl.multiple_of(p * CHUNK, CHUNK), CHUNK), :], stage.at[p % 2], stsem.at[p % 2]
        )

    def load_cross(p):
        return pltpu.make_async_copy(
            xm.at[0, :, pl.ds(pl.multiple_of(p * CHUNK, CHUNK), CHUNK)], xstage.at[p % 2], stsem.at[2 + p % 2]
        )

    load_own = pltpu.make_async_copy(amp, own, lsem)
    load_own.start()
    load_ladder(0).start()
    load_cross(0).start()

    barrier = pltpu.get_barrier_semaphore()
    partners = [(row_dev(i), c) for i in range(7)] + [sibling, above, below, beside]
    for device in partners:
        pl.semaphore_signal(barrier, inc=1, device_id=device, device_id_type=MESH)
    load_own.wait()
    gath[r, 0:rows, :] = own[...]
    gath[r, rows:PAD, :] = jnp.zeros((PAD - rows, width), F32)
    pl.semaphore_wait(barrier, len(partners))

    def hop(i, shard, device, columns=None):
        ref = gath.at[shard] if columns is None else gath.at[shard, :, pl.ds(columns, half)]
        return remote(ref, ref, gs.at[i], gr.at[i], device)

    g1, g2, g3 = hop(0, r, right), hop(1, r, left), hop(2, r, across)
    g1.start()
    g2.start()
    g3.start()
    mcopies = []
    for i in range(7):
        copy = remote(meta.at[row_dev(i)], mrecv.at[r], ms.at[i], mr.at[i], (row_dev(i), c))
        copy.start()
        mcopies.append(copy)
    mrecv[r] = meta[r]

    @pl.loop(0, 2 * chunks)
    def _(p):
        load_ladder(p).wait()

        @pl.when(p + 1 < 2 * chunks)
        def _():
            load_ladder(p + 1).start()

        high, low = split(stage[p % 2])
        chi[p] = high
        clo[p] = low

    slots = NROW * CAP
    pairs = [
        (r, x * 2 + 1 - yh),
        (xm1 * 2 + yh, xp * 2 + yh),
        (x2 * 2 + yh, xm1 * 2 + 1 - yh),
        (xp * 2 + 1 - yh, x2 * 2 + 1 - yh),
    ]
    units = [shard for pair in pairs for shard in pair]
    group = 2 * PAD

    def place(g, shape, axis):
        index = lax.broadcasted_iota(jnp.int32, shape, axis)
        return jnp.where(index < PAD, index + pairs[g][0] * PAD, index + (pairs[g][1] - 1) * PAD).astype(F32)

    def convert(g):
        high, low = split(jnp.concatenate([gath[pairs[g][0]], gath[pairs[g][1]]], axis=0))
        ahi[g] = high
        alo[g] = low

    def take(g):
        chosen = jnp.where(place(g, (slots, group), 1) == colb[:, 0:1], 1.0, 0.0).astype(BF16)
        for n in range(chunks):
            columns = slice(n * CHUNK, (n + 1) * CHUNK)
            part = dot(chosen, ahi[g, :, columns]) + dot(chosen, alo[g, :, columns])
            if g == 0:
                pacc[:, columns] = part
            else:
                pacc[:, columns] += part

    def ladder(s, k, target, h):
        p = s * chunks + k
        high = ahi[2 * h : 2 * h + 2].reshape(2 * group, width)
        low = alo[2 * h : 2 * h + 2].reshape(2 * group, width)
        value = dot_t(high, chi[p]) + dot_t(low, chi[p]) + dot_t(high, clo[p])
        for i in range(4):
            target[units[4 * h + i]] = value[i * PAD : (i + 1) * PAD]

    def early(k):
        ladder(1 - core, k, sib.at[k], 0)
        ladder(core, k, mine.at[k], 0)

    n_left, n_right, n_across, n_far = xm1 * 2 + yh, xp * 2 + yh, x * 2 + 1 - yh, x2 * 2 + yh
    hop(0, n_left, right).wait_recv()
    g4 = hop(3, n_left, right, 0)
    g4.start()
    hop(1, n_right, left).wait_recv()
    g5 = hop(4, n_right, left, half)
    g5.start()
    convert(1)
    hop(2, n_across, across).wait_recv()
    convert(0)

    @pl.loop(0, 2)
    def _(k):
        early(k)

    g4.wait_send()
    g5.wait_send()
    g6, g7 = hop(5, n_across, right), hop(6, n_across, left)
    g6.start()
    g7.start()
    hop(3, n_far, right, 0).wait_recv()
    hop(4, n_far, left, half).wait_recv()
    g8 = hop(7, n_far, across)
    g8.start()

    @pl.loop(2, chunks)
    def _(k):
        early(k)

    @pl.loop(0, chunks)
    def _(p):
        load_cross(p).wait()

        @pl.when(p + 1 < chunks)
        def _():
            load_cross(p + 1).start()

        high, low = split(xstage[p % 2])
        xhi[p] = high
        xlo[p] = low

    for i in range(7):
        remote(meta.at[r], mrecv.at[row_src(i)], ms.at[i], mr.at[i], (row_src(i), c)).wait_recv()
    diagonal = lax.broadcasted_iota(jnp.int32, (CAP, 128), 0) == lax.broadcasted_iota(jnp.int32, (CAP, 128), 1)
    for s in range(NROW):
        for row, target in ((0, colb), (1, colc)):
            column = jnp.sum(jnp.where(diagonal, mrecv[s, row : row + 1, :], 0.0), axis=1, keepdims=True)
            target[s * CAP : (s + 1) * CAP, :] = jnp.broadcast_to(column, (CAP, 128))
    take(0)
    take(1)
    for s in range(2):
        for g in range(4):
            hit = jnp.where(place(g, (group, slots), 0) == tgt[s : s + 1, 0:slots], 1.0, 0.0)
            onehot[s, g] = hit.astype(BF16)

    hop(5, xm1 * 2 + 1 - yh, right).wait_recv()
    convert(2)
    take(2)
    hop(6, xp * 2 + 1 - yh, left).wait_recv()
    hop(7, x2 * 2 + 1 - yh, across).wait_recv()
    convert(3)
    take(3)
    for n in range(chunks):
        columns = slice(n * CHUNK, (n + 1) * CHUNK)
        high, low = split(pacc[:, columns] * colc[:, 0:1])
        phi[:, columns] = high
        plo[:, columns] = low

    def returned(k, i, source):
        return remote(cross.at[k, source], back.at[k, r], ts.at[k, i], tr.at[k, i], (source, c))

    def product(k):
        value = dot(phi[...], xhi[k]) + dot(plo[...], xhi[k]) + dot(phi[...], xlo[k])
        cross[k] = value.reshape(NROW, CAP, CHUNK)
        for i in range(7):
            returned(k, i, row_dev(i)).start()
        back[k, r] = cross[k, r]

    def scatter(s, k, target):
        high, low = split(back[k].reshape(slots, CHUNK))
        hits = onehot[s].reshape(4 * group, slots)
        value = dot(hits, high) + dot(hits, low)
        for i in range(8):
            target[units[i]] += value[i * PAD : (i + 1) * PAD]

    def to_sibling(k):
        return remote(sib.at[k], crecv.at[k], cs.at[k], cr.at[k], sibling)

    def unit(k, depth, side):
        return mine.at[k, side * 4 + depth]

    quarter = CHUNK // 2

    def around(k, i):
        source, target, device = [
            (unit(k, zp, 1 - yl), zrecv.at[k, 0], above),
            (unit(k, zm, 1 - yl), zrecv.at[k, 1], below),
            (unit(k, z2, yl).at[:, 0:quarter], hrecv.at[k, 0], above),
            (unit(k, z2, yl).at[:, quarter:CHUNK], hrecv.at[k, 1], below),
            (unit(k, zp, yl), zrecv.at[k, 2], above),
            (unit(k, zm, yl), zrecv.at[k, 3], below),
        ][i]
        return remote(source, target, zs.at[k, i], zr.at[k, i], device)

    def aside(k, i):
        return remote(unit(k, z if i else z2, 1 - yl), yrecv.at[k, i], ys.at[k, i], yr.at[k, i], beside)

    def exchange(k):
        return remote(esend.at[k], erecv.at[k], es.at[k], er.at[k], sibling)

    product(0)
    block = rows // 2
    same, other = yl * 4, (1 - yl) * 4

    @pl.loop(0, chunks + 3)
    def _(t):
        @pl.when(t < chunks)
        def _():
            @pl.when(t + 1 < chunks)
            def _():
                product(t + 1)

            ladder(1 - core, t, sib.at[t], 1)
            for i in range(7):
                remote(
                    cross.at[t, r], back.at[t, row_src(i)], ts.at[t, i], tr.at[t, i], (row_src(i), c)
                ).wait_recv()
            scatter(1 - core, t, sib.at[t])
            to_sibling(t).start()

        @pl.when((t >= 1) & (t < chunks + 1))
        def _():
            k = t - 1
            aside(k, 0).wait_recv()
            mine[k, same + z2] += yrecv[k, 0]
            around(k, 2).start()
            around(k, 3).start()

        @pl.when(t < chunks)
        def _():
            ladder(core, t, mine.at[t], 1)
            scatter(core, t, mine.at[t])
            to_sibling(t).wait_recv()
            mine[t] += crecv[t]
            aside(t, 0).start()
            around(t, 0).start()
            around(t, 1).start()

        @pl.when((t >= 1) & (t < chunks + 1))
        def _():
            k = t - 1
            around(k, 2).wait_recv()
            mine[k, same + zp, :, 0:quarter] += hrecv[k, 0]
            around(k, 4).start()
            around(k, 3).wait_recv()
            mine[k, same + zm, :, quarter:CHUNK] += hrecv[k, 1]
            around(k, 5).start()
            around(k, 0).wait_recv()
            around(k, 1).wait_recv()
            mine[k, other + z] += zrecv[k, 0] + zrecv[k, 1]
            aside(k, 1).start()

        @pl.when((t >= 2) & (t < chunks + 2))
        def _():
            k = t - 2
            around(k, 4).wait_recv()
            around(k, 5).wait_recv()
            aside(k, 1).wait_recv()
            mine[k, same + z] += zrecv[k, 2] + zrecv[k, 3] + yrecv[k, 1]
            low = mine[k, same + z, 0:block, :]
            high = mine[k, same + z, block:rows, :]
            esend[k] = jnp.where(core == 0, high, low)
            exchange(k).start()
            out[:, pl.ds(pl.multiple_of(core * width + k * CHUNK, CHUNK), CHUNK)] = jnp.where(core == 0, low, high)

        @pl.when(t >= 3)
        def _():
            k = t - 3
            exchange(k).wait_recv()
            out[:, pl.ds(pl.multiple_of((1 - core) * width + k * CHUNK, CHUNK), CHUNK)] = erecv[k]

    for copy in [g1, g2, g3, g6, g7, g8] + mcopies:
        copy.wait_send()

    @pl.loop(0, chunks)
    def _(k):
        for i in range(7):
            returned(k, i, row_dev(i)).wait_send()
        to_sibling(k).wait_send()
        for i in range(6):
            around(k, i).wait_send()
        aside(k, 0).wait_send()
        aside(k, 1).wait_send()
        exchange(k).wait_send()


def tables(channel_slot, channel_of, source_row, target_row, recoupling, shard):
    names = jnp.arange(NROW, dtype=jnp.int32)
    named = channel_of[0] == names[None, :]
    owners = jnp.sum(jnp.where(named, channel_slot[None, :], 0), axis=1)
    marks = (owners[:, None] == names[None, :]).astype(jnp.int32)
    before = jnp.cumsum(marks, axis=0) - marks
    slot = owners * CAP + jnp.sum(before * marks, axis=1)
    match = slot[None, :] == jnp.arange(NROW * CAP, dtype=jnp.int32)[:, None]
    pad = PAD - shard
    source = source_row[0] + pad * (source_row[0] // shard)
    hole = target_row[0] // 2
    hole = hole + pad * (hole // shard)
    odd = target_row[0] % 2

    def place(value, where):
        return (jnp.sum(jnp.where(where, value[None, :] + 1, 0), axis=1) - 1).astype(F32)

    chosen = place(source, match)
    scale = jnp.sum(jnp.where(match, recoupling[0][None, :], 0.0), axis=1)
    even_target = place(hole, match & (odd == 0)[None, :])
    odd_target = place(hole, match & (odd == 1)[None, :])
    meta = jnp.stack([chosen.reshape(NROW, CAP), scale.reshape(NROW, CAP)], axis=1)
    meta = jnp.pad(meta, ((0, 0), (0, 6), (0, 128 - CAP)))
    return meta, jnp.stack([even_target, odd_target])


def on_device(
    amplitude,
    ladder_coupling,
    crossed_coupling,
    channel_slot,
    channel_of,
    source_row,
    target_row,
    recoupling,
    driving,
    denominator,
):
    rows, width = amplitude.shape
    chunks = width // CHUNK
    slots = NROW * CAP
    group = 2 * PAD
    meta, tgt = tables(channel_slot, channel_of, source_row, target_row, recoupling, rows)
    dma = pltpu.SemaphoreType.DMA
    vmem = pltpu.VMEM
    summed = pl.pallas_call(
        kernel,
        out_shape=jax.ShapeDtypeStruct((rows // 2, 2 * width), F32),
        in_specs=[pl.BlockSpec(memory_space=pltpu.VMEM)] * 2 + [pl.BlockSpec(memory_space=pl.ANY)] * 3,
        out_specs=pl.BlockSpec(memory_space=pltpu.VMEM),
        scratch_shapes=[
            vmem((rows, width), F32),
            vmem((NROW, PAD, width), F32),
            vmem((4, group, width), BF16),
            vmem((4, group, width), BF16),
            vmem((2, CHUNK, width), F32),
            vmem((2 * chunks, CHUNK, width), BF16),
            vmem((2 * chunks, CHUNK, width), BF16),
            vmem((2, width, CHUNK), F32),
            vmem((chunks, width, CHUNK), BF16),
            vmem((chunks, width, CHUNK), BF16),
            vmem((NROW, 8, 128), F32),
            vmem((slots, 128), F32),
            vmem((slots, 128), F32),
            vmem((slots, width), F32),
            vmem((slots, width), BF16),
            vmem((slots, width), BF16),
            vmem((2, 4, group, slots), BF16),
            vmem((chunks, NROW, CAP, CHUNK), F32),
            vmem((chunks, NROW, CAP, CHUNK), F32),
            vmem((chunks, NROW, PAD, CHUNK), F32),
            vmem((chunks, NROW, PAD, CHUNK), F32),
            vmem((chunks, NROW, PAD, CHUNK), F32),
            vmem((chunks, 4, PAD, CHUNK), F32),
            vmem((chunks, 2, PAD, CHUNK // 2), F32),
            vmem((chunks, 2, PAD, CHUNK), F32),
            vmem((chunks, rows // 2, CHUNK), F32),
            vmem((chunks, rows // 2, CHUNK), F32),
            dma,
            dma((4,)),
            dma((8,)),
            dma((8,)),
            dma((7,)),
            dma((7,)),
            dma((chunks, 7)),
            dma((chunks, 7)),
            dma((chunks,)),
            dma((chunks,)),
            dma((chunks, 6)),
            dma((chunks, 6)),
            dma((chunks, 2)),
            dma((chunks, 2)),
            dma((chunks,)),
            dma((chunks,)),
        ],
        compiler_params=pltpu.CompilerParams(
            collective_id=0, has_side_effects=True, vmem_limit_bytes=63 * 1024 * 1024
        ),
        cost_estimate=pl.CostEstimate(flops=24_000_000_000, bytes_accessed=22_000_000, transcendentals=0),
    )(meta, tgt, amplitude, ladder_coupling, crossed_coupling)
    return (driving + summed) / denominator


def solution(mesh):
    in_specs = (
        P("row", "col"),
        P("row", "col"),
        P("row", None, None),
        P(),
        P("col", "row", None),
        P("col", "row"),
        P("col", "row"),
        P("col", "row"),
        P("col", "row"),
        P("col", "row"),
    )
    out_specs = P("col", "row")
    return jax.shard_map(
        on_device, mesh=mesh, in_specs=in_specs, out_specs=out_specs, check_vma=False
    )
```

```python
import jax
import jax.numpy as jnp
from jax import lax
from jax.experimental import pallas as pl
from jax.experimental.pallas import tpu as pltpu
from jax.sharding import PartitionSpec as P

CAP = 40
NROW = 8
PAD = 104
CHUNK = 256
MESH = pl.DeviceIdType.MESH
F32 = jnp.float32
BF16 = jnp.bfloat16
OFFSETS = [(dx, dy) for dx in (1, 3, 2, 0) for dy in (0, 1) if (dx, dy) != (0, 0)]


def split(value):
    high = value.astype(BF16)
    return high, (value - high.astype(F32)).astype(BF16)


def dot(a, b):
    return lax.dot_general(a, b, (((1,), (0,)), ((), ())), preferred_element_type=F32)


def dot_t(a, b):
    return lax.dot_general(a, b, (((1,), (1,)), ((), ())), preferred_element_type=F32)


def kernel(
    channel_slot, channel_of, source_row, target_row, recoupling, amp, lad, xm, driving, denominator, out,
    own, gath, ahi, alo, stage, chi, clo, xstage, xhi, xlo, meta, mrecv, tgt, tsib, tall, colb, colc, pacc, phi, plo,
    onehot, cross, back, bsib, sib, mine, crecv, zrecv, yrecv, esend, erecv, drv, den,
    lsem, stsem, gs, gr, ms, mr, ts, tr, bs, br, cs, cr, zs, zr, ys, yr, es, er,
):
    rows, width = amp.shape
    chunks = width // CHUNK
    half = width // 2
    r, c = lax.axis_index("row"), lax.axis_index("col")
    x, yh = r // 2, r % 2
    yl, z, core = c // 8, (c // 2) % 4, c % 2
    xp, xm1, x2 = (x + 1) % 4, (x + 3) % 4, (x + 2) % 4
    zp, zm, z2 = (z + 1) % 4, (z + 3) % 4, (z + 2) % 4

    def row_dev(i):
        dx, dy = OFFSETS[i]
        return ((x + dx) % 4) * 2 + (yh + dy) % 2

    def row_src(i):
        dx, dy = OFFSETS[i]
        return ((x + 4 - dx) % 4) * 2 + (yh + dy) % 2

    sibling = (r, yl * 8 + z * 2 + (1 - core))
    above = (r, yl * 8 + zp * 2 + core)
    below = (r, yl * 8 + zm * 2 + core)
    beside = (r, (1 - yl) * 8 + z * 2 + core)
    right, left, across = (xp * 2 + yh, c), (xm1 * 2 + yh, c), (x * 2 + 1 - yh, c)

    def remote(src, dst, send, recv, device):
        return pltpu.make_async_remote_copy(
            src_ref=src, dst_ref=dst, send_sem=send, recv_sem=recv, device_id=device, device_id_type=MESH
        )

    def load_ladder(p):
        return pltpu.make_async_copy(
            lad.at[pl.ds(pl.multiple_of(p * CHUNK, CHUNK), CHUNK), :], stage.at[p % 2], stsem.at[p % 2]
        )

    def load_cross(p):
        return pltpu.make_async_copy(
            xm.at[0, :, pl.ds(pl.multiple_of(p * CHUNK, CHUNK), CHUNK)], xstage.at[p % 2], stsem.at[2 + p % 2]
        )

    load_own = pltpu.make_async_copy(amp, own, lsem.at[0])
    load_drv = pltpu.make_async_copy(driving, drv, lsem.at[1])
    load_den = pltpu.make_async_copy(denominator, den, lsem.at[2])
    load_own.start()
    load_ladder(0).start()
    load_cross(0).start()
    load_drv.start()
    load_den.start()

    barrier = pltpu.get_barrier_semaphore()
    partners = [(row_dev(i), c) for i in range(7)] + [sibling, above, below, beside]
    for device in partners:
        pl.semaphore_signal(barrier, inc=1, device_id=device, device_id_type=MESH)
    load_own.wait()
    gath[r, 0:rows, :] = own[...]
    gath[r, rows:PAD, :] = jnp.zeros((PAD - rows, width), F32)
    tables(rows, channel_slot, channel_of, source_row, target_row, recoupling, meta, tgt)
    pl.semaphore_wait(barrier, len(partners))

    def hop(i, shard, device, columns=None):
        ref = gath.at[shard] if columns is None else gath.at[shard, :, pl.ds(columns, half)]
        return remote(ref, ref, gs.at[i], gr.at[i], device)

    g1, g2, g3 = hop(0, r, right), hop(1, r, left), hop(2, r, across)
    g1.start()
    g2.start()
    g3.start()
    mcopies = []
    for i in range(7):
        copy = remote(meta.at[row_dev(i)], mrecv.at[r], ms.at[i], mr.at[i], (row_dev(i), c))
        copy.start()
        mcopies.append(copy)
    tcopy = remote(tgt, tsib, ms.at[7], mr.at[7], sibling)
    tcopy.start()
    mrecv[r] = meta[r]

    @pl.loop(0, 2 * chunks)
    def _(p):
        load_ladder(p).wait()

        @pl.when(p + 1 < 2 * chunks)
        def _():
            load_ladder(p + 1).start()

        high, low = split(stage[p % 2])
        chi[p] = high
        clo[p] = low

    slots = NROW * CAP
    pairs = [
        (r, x * 2 + 1 - yh),
        (xm1 * 2 + yh, xp * 2 + yh),
        (x2 * 2 + yh, xm1 * 2 + 1 - yh),
        (xp * 2 + 1 - yh, x2 * 2 + 1 - yh),
    ]
    units = [shard for pair in pairs for shard in pair]
    group = 2 * PAD

    def place(g, shape, axis):
        index = lax.broadcasted_iota(jnp.int32, shape, axis)
        return jnp.where(index < PAD, index + pairs[g][0] * PAD, index + (pairs[g][1] - 1) * PAD).astype(F32)

    def convert(g):
        high, low = split(jnp.concatenate([gath[pairs[g][0]], gath[pairs[g][1]]], axis=0))
        ahi[g] = high
        alo[g] = low

    def take(g):
        chosen = jnp.where(place(g, (slots, group), 1) == colb[:, 0:1], 1.0, 0.0).astype(BF16)
        for n in range(chunks):
            columns = slice(n * CHUNK, (n + 1) * CHUNK)
            part = dot(chosen, ahi[g, :, columns]) + dot(chosen, alo[g, :, columns])
            if g == 0:
                pacc[:, columns] = part
            else:
                pacc[:, columns] += part

    def ladder(s, k, target, h):
        p = s * chunks + k
        high = ahi[2 * h : 2 * h + 2].reshape(2 * group, width)
        low = alo[2 * h : 2 * h + 2].reshape(2 * group, width)
        value = dot_t(high, chi[p]) + dot_t(low, chi[p]) + dot_t(high, clo[p])
        for i in range(4):
            target[units[4 * h + i]] = value[i * PAD : (i + 1) * PAD]

    def both(k, h):
        ladder(1 - core, k, sib.at[k], h)
        ladder(core, k, mine.at[k], h)

    n_left, n_right, n_across, n_far = xm1 * 2 + yh, xp * 2 + yh, x * 2 + 1 - yh, x2 * 2 + yh
    hop(0, n_left, right).wait_recv()
    g4 = hop(3, n_left, right, 0)
    g4.start()
    hop(1, n_right, left).wait_recv()
    g5 = hop(4, n_right, left, half)
    g5.start()
    convert(1)
    hop(2, n_across, across).wait_recv()
    convert(0)

    @pl.loop(0, 2)
    def _(k):
        both(k, 0)

    g4.wait_send()
    g5.wait_send()
    g6, g7 = hop(5, n_across, right), hop(6, n_across, left)
    g6.start()
    g7.start()
    hop(3, n_far, right, 0).wait_recv()
    hop(4, n_far, left, half).wait_recv()
    g8 = hop(7, n_far, across)
    g8.start()

    @pl.loop(2, chunks)
    def _(k):
        both(k, 0)

    @pl.loop(0, chunks)
    def _(p):
        load_cross(p).wait()

        @pl.when(p + 1 < chunks)
        def _():
            load_cross(p + 1).start()

        high, low = split(xstage[p % 2])
        xhi[p] = high
        xlo[p] = low

    for i in range(7):
        remote(meta.at[r], mrecv.at[row_src(i)], ms.at[i], mr.at[i], (row_src(i), c)).wait_recv()
    diagonal = lax.broadcasted_iota(jnp.int32, (CAP, 128), 0) == lax.broadcasted_iota(jnp.int32, (CAP, 128), 1)
    for s in range(NROW):
        for row, target in ((0, colb), (1, colc)):
            column = jnp.sum(jnp.where(diagonal, mrecv[s, row : row + 1, :], 0.0), axis=1, keepdims=True)
            target[s * CAP : (s + 1) * CAP, :] = jnp.broadcast_to(column, (CAP, 128))
    take(0)
    take(1)
    tcopy.wait_recv()
    tall[:, 0:slots] = tgt[pl.ds(core, 1), :]
    tall[:, slots : 2 * slots] = tsib[pl.ds(core, 1), :]
    for g in range(4):
        hit = jnp.where(place(g, (group, 2 * slots), 0) == tall[...], 1.0, 0.0)
        onehot[g] = hit.astype(BF16)

    hop(5, xm1 * 2 + 1 - yh, right).wait_recv()
    convert(2)
    take(2)
    hop(6, xp * 2 + 1 - yh, left).wait_recv()
    hop(7, x2 * 2 + 1 - yh, across).wait_recv()
    convert(3)
    take(3)
    for n in range(chunks):
        columns = slice(n * CHUNK, (n + 1) * CHUNK)
        high, low = split(pacc[:, columns] * colc[:, 0:1])
        phi[:, columns] = high
        plo[:, columns] = low

    def returned(k, i, source):
        return remote(cross.at[k, source], back.at[k, r], ts.at[k, i], tr.at[k, i], (source, c))

    def product(k):
        value = dot(phi[...], xhi[k]) + dot(plo[...], xhi[k]) + dot(phi[...], xlo[k])
        cross[k] = value.reshape(NROW, CAP, CHUNK)
        for i in range(7):
            returned(k, i, row_dev(i)).start()
        back[k, r] = cross[k, r]

    def scatter(k):
        high, low = split(jnp.concatenate([back[k].reshape(slots, CHUNK), bsib[k].reshape(slots, CHUNK)], axis=0))
        hits = onehot[...].reshape(4 * group, 2 * slots)
        value = dot(hits, high) + dot(hits, low)
        for i in range(8):
            mine[k, units[i]] += value[i * PAD : (i + 1) * PAD] + crecv[k, units[i]]

    def to_sibling(k):
        return remote(sib.at[k], crecv.at[k], cs.at[k], cr.at[k], sibling)

    def unit(k, depth, side):
        return mine.at[k, side * 4 + depth]

    def pass_on(k):
        return remote(back.at[k], bsib.at[k], bs.at[k], br.at[k], sibling)

    def around(k, i):
        source, device = [
            (unit(k, z2, 0), above),
            (unit(k, z2, 1), below),
            (unit(k, zp, 1), above),
            (unit(k, zm, 0), below),
            (unit(k, zp, 0), above),
            (unit(k, zm, 1), below),
        ][i]
        return remote(source, zrecv.at[k, i], zs.at[k, i], zr.at[k, i], device)

    def aside(k):
        return remote(unit(k, z, 1 - yl), yrecv.at[k], ys.at[k], yr.at[k], beside)

    def exchange(k):
        return remote(esend.at[k], erecv.at[k], es.at[k], er.at[k], sibling)

    def solve(k, half_index, value):
        columns = pl.ds(pl.multiple_of(half_index * width + k * CHUNK, CHUNK), CHUNK)
        out[:, columns] = (drv[:, columns] + value) / den[:, columns]

    def late(k):
        ladder(1 - core, k, sib.at[k], 1)
        to_sibling(k).start()
        ladder(core, k, mine.at[k], 1)

    product(0)
    product(1)
    late(0)
    load_drv.wait()
    load_den.wait()
    block = rows // 2
    final = yl * 4 + z

    @pl.loop(0, chunks + 4)
    def _(t):
        @pl.when(t < chunks)
        def _():
            for i in range(7):
                remote(
                    cross.at[t, r], back.at[t, row_src(i)], ts.at[t, i], tr.at[t, i], (row_src(i), c)
                ).wait_recv()
            pass_on(t).start()

            @pl.when(t + 2 < chunks)
            def _():
                product(t + 2)

        @pl.when(t + 1 < chunks)
        def _():
            late(t + 1)

        @pl.when(t < chunks)
        def _():
            to_sibling(t).wait_recv()
            pass_on(t).wait_recv()
            scatter(t)
            for i in range(4):
                around(t, i).start()

        @pl.when((t >= 1) & (t < chunks + 1))
        def _():
            k = t - 1
            around(k, 0).wait_recv()
            mine[k, zp] += zrecv[k, 0]
            around(k, 4).start()
            around(k, 1).wait_recv()
            mine[k, 4 + zm] += zrecv[k, 1]
            around(k, 5).start()

        @pl.when((t >= 2) & (t < chunks + 2))
        def _():
            k = t - 2
            for i in range(2, 6):
                around(k, i).wait_recv()
            mine[k, z] += zrecv[k, 3] + zrecv[k, 4]
            mine[k, 4 + z] += zrecv[k, 2] + zrecv[k, 5]
            aside(k).start()

        @pl.when((t >= 3) & (t < chunks + 3))
        def _():
            k = t - 3
            aside(k).wait_recv()
            mine[k, final] += yrecv[k]
            low = mine[k, final, 0:block, :]
            high = mine[k, final, block:rows, :]
            esend[k] = jnp.where(core == 0, high, low)
            exchange(k).start()
            solve(k, core, jnp.where(core == 0, low, high))

        @pl.when(t >= 4)
        def _():
            k = t - 4
            exchange(k).wait_recv()
            solve(k, 1 - core, erecv[k])

    for copy in [g1, g2, g3, g6, g7, g8, tcopy] + mcopies:
        copy.wait_send()

    @pl.loop(0, chunks)
    def _(k):
        for i in range(7):
            returned(k, i, row_dev(i)).wait_send()
        to_sibling(k).wait_send()
        for i in range(6):
            around(k, i).wait_send()
        aside(k).wait_send()
        pass_on(k).wait_send()
        exchange(k).wait_send()


def tables(shard, channel_slot, channel_of, source_row, target_row, recoupling, meta, tgt):
    items = channel_of.shape[1]
    channel = channel_of[...]
    owner = jnp.zeros(channel.shape, jnp.int32)
    for i in range(NROW):
        owner = jnp.where(channel == i, channel_slot[i], owner)
    marks = jnp.where(lax.broadcasted_iota(jnp.int32, (NROW, items), 0) == owner, 1.0, 0.0)
    square = (items, items)
    down, along = lax.broadcasted_iota(jnp.int32, square, 0), lax.broadcasted_iota(jnp.int32, square, 1)
    before = dot(marks.astype(BF16), jnp.where(down < along, 1.0, 0.0).astype(BF16))
    slot = owner.astype(F32) * CAP + jnp.sum(marks * before, axis=0, keepdims=True)

    def padded(row):
        passed = row
        for i in range(1, NROW):
            passed = passed + jnp.where(row >= i * shard, PAD - shard, 0)
        return passed.astype(F32)

    def column(row):
        return jnp.sum(jnp.where(down == along, row, 0.0), axis=1, keepdims=True)

    target = target_row[...]
    slot_c, scale_c = column(slot), column(recoupling[...])
    source_c, hole_c = column(padded(source_row[...])), column(padded(target >> 1))
    odd_c = column((target & 1).astype(F32))
    lanes = along.astype(F32)
    for i in range(NROW):
        match = slot_c == lanes + i * CAP
        meta[i, 0:1, :] = jnp.sum(jnp.where(match, source_c + 1.0, 0.0), axis=0, keepdims=True) - 1.0
        meta[i, 1:2, :] = jnp.sum(jnp.where(match, scale_c, 0.0), axis=0, keepdims=True)
        meta[i, 2:8, :] = jnp.zeros((6, items), F32)
    slots = NROW * CAP
    match = slot_c == lax.broadcasted_iota(jnp.int32, (items, slots), 1).astype(F32)
    for i in range(2):
        hit = match & (odd_c == float(i))
        tgt[i : i + 1, :] = jnp.sum(jnp.where(hit, hole_c + 1.0, 0.0), axis=0, keepdims=True) - 1.0


def on_device(
    amplitude,
    ladder_coupling,
    crossed_coupling,
    channel_slot,
    channel_of,
    source_row,
    target_row,
    recoupling,
    driving,
    denominator,
):
    rows, width = amplitude.shape
    chunks = width // CHUNK
    slots = NROW * CAP
    group = 2 * PAD
    dma = pltpu.SemaphoreType.DMA
    vmem = pltpu.VMEM
    return pl.pallas_call(
        kernel,
        out_shape=jax.ShapeDtypeStruct((rows // 2, 2 * width), F32),
        in_specs=[pl.BlockSpec(memory_space=pltpu.SMEM)]
        + [pl.BlockSpec(memory_space=pltpu.VMEM)] * 4
        + [pl.BlockSpec(memory_space=pl.ANY)] * 5,
        out_specs=pl.BlockSpec(memory_space=pltpu.VMEM),
        scratch_shapes=[
            vmem((rows, width), F32),
            vmem((NROW, PAD, width), F32),
            vmem((4, group, width), BF16),
            vmem((4, group, width), BF16),
            vmem((2, CHUNK, width), F32),
            vmem((2 * chunks, CHUNK, width), BF16),
            vmem((2 * chunks, CHUNK, width), BF16),
            vmem((2, width, CHUNK), F32),
            vmem((chunks, width, CHUNK), BF16),
            vmem((chunks, width, CHUNK), BF16),
            vmem((NROW, 8, 128), F32),
            vmem((NROW, 8, 128), F32),
            vmem((2, slots), F32),
            vmem((2, slots), F32),
            vmem((1, 2 * slots), F32),
            vmem((slots, 128), F32),
            vmem((slots, 128), F32),
            vmem((slots, width), F32),
            vmem((slots, width), BF16),
            vmem((slots, width), BF16),
            vmem((4, group, 2 * slots), BF16),
            vmem((chunks, NROW, CAP, CHUNK), F32),
            vmem((chunks, NROW, CAP, CHUNK), F32),
            vmem((chunks, NROW, CAP, CHUNK), F32),
            vmem((chunks, NROW, PAD, CHUNK), F32),
            vmem((chunks, NROW, PAD, CHUNK), F32),
            vmem((chunks, NROW, PAD, CHUNK), F32),
            vmem((chunks, 6, PAD, CHUNK), F32),
            vmem((chunks, PAD, CHUNK), F32),
            vmem((chunks, rows // 2, CHUNK), F32),
            vmem((chunks, rows // 2, CHUNK), F32),
            vmem((rows // 2, 2 * width), F32),
            vmem((rows // 2, 2 * width), F32),
            dma((3,)),
            dma((4,)),
            dma((8,)),
            dma((8,)),
            dma((8,)),
            dma((8,)),
            dma((chunks, 7)),
            dma((chunks, 7)),
            dma((chunks,)),
            dma((chunks,)),
            dma((chunks,)),
            dma((chunks,)),
            dma((chunks, 6)),
            dma((chunks, 6)),
            dma((chunks,)),
            dma((chunks,)),
            dma((chunks,)),
            dma((chunks,)),
        ],
        compiler_params=pltpu.CompilerParams(
            collective_id=0, has_side_effects=True, vmem_limit_bytes=63 * 1024 * 1024
        ),
        cost_estimate=pl.CostEstimate(flops=24_000_000_000, bytes_accessed=22_000_000, transcendentals=0),
    )(
        channel_slot,
        channel_of.reshape(1, -1),
        source_row,
        target_row,
        recoupling,
        amplitude,
        ladder_coupling,
        crossed_coupling,
        driving,
        denominator,
    )


def solution(mesh):
    in_specs = (
        P("row", "col"),
        P("row", "col"),
        P("row", None, None),
        P(),
        P("col", "row", None),
        P("col", "row"),
        P("col", "row"),
        P("col", "row"),
        P("col", "row"),
        P("col", "row"),
    )
    out_specs = P("col", "row")
    return jax.shard_map(
        on_device, mesh=mesh, in_specs=in_specs, out_specs=out_specs, check_vma=False
    )
```

```python
import jax
import jax.numpy as jnp
from jax import lax
from jax.experimental import pallas as pl
from jax.experimental.pallas import tpu as pltpu
from jax.sharding import PartitionSpec as P

CAP = 40
NROW = 8
FAR = 3
PAD = 104
CHUNK = 256
MESH = pl.DeviceIdType.MESH
F32 = jnp.float32
BF16 = jnp.bfloat16
OFFSETS = [(dx, dy) for dx in (1, 3, 2, 0) for dy in (0, 1) if (dx, dy) != (0, 0)]


def split(value):
    high = value.astype(BF16)
    return high, (value - high.astype(F32)).astype(BF16)


def dot(a, b):
    return lax.dot_general(a, b, (((1,), (0,)), ((), ())), preferred_element_type=F32)


def dot_t(a, b):
    return lax.dot_general(a, b, (((1,), (1,)), ((), ())), preferred_element_type=F32)


def kernel(
    channel_slot, channel_of, source_row, target_row, recoupling, amp, lad, xm, driving, denominator, out,
    own, gath, ahi, alo, stage, chi, clo, xstage, xhi, xlo, meta, mrecv, tgt, tsib, tall, colb, colc, pacc, phi, plo,
    onehot, cross, back, bsib, sib, mine, crecv, zrecv, yrecv, esend, erecv, drv, den,
    lsem, stsem, gs, gr, ms, mr, ts, tr, bs, br, cs, cr, zs, zr, ys, yr, es, er,
):
    rows, width = amp.shape
    chunks = width // CHUNK
    half = width // 2
    r, c = lax.axis_index("row"), lax.axis_index("col")
    x, yh = r // 2, r % 2
    yl, z, core = c // 8, (c // 2) % 4, c % 2
    xp, xm1, x2 = (x + 1) % 4, (x + 3) % 4, (x + 2) % 4
    zp, zm, z2 = (z + 1) % 4, (z + 3) % 4, (z + 2) % 4

    def row_dev(i):
        dx, dy = OFFSETS[i]
        return ((x + dx) % 4) * 2 + (yh + dy) % 2

    def row_src(i):
        dx, dy = OFFSETS[i]
        return ((x + 4 - dx) % 4) * 2 + (yh + dy) % 2

    sibling = (r, yl * 8 + z * 2 + (1 - core))
    above = (r, yl * 8 + zp * 2 + core)
    below = (r, yl * 8 + zm * 2 + core)
    beside = (r, (1 - yl) * 8 + z * 2 + core)
    right, left, across = (xp * 2 + yh, c), (xm1 * 2 + yh, c), (x * 2 + 1 - yh, c)

    def remote(src, dst, send, recv, device):
        return pltpu.make_async_remote_copy(
            src_ref=src, dst_ref=dst, send_sem=send, recv_sem=recv, device_id=device, device_id_type=MESH
        )

    def load_ladder(p):
        return pltpu.make_async_copy(
            lad.at[pl.ds(pl.multiple_of(p * CHUNK, CHUNK), CHUNK), :], stage.at[p % 2], stsem.at[p % 2]
        )

    def load_cross(p):
        return pltpu.make_async_copy(
            xm.at[0, :, pl.ds(pl.multiple_of(p * CHUNK, CHUNK), CHUNK)], xstage.at[p % 2], stsem.at[2 + p % 2]
        )

    load_own = pltpu.make_async_copy(amp, own, lsem.at[0])
    load_drv = pltpu.make_async_copy(driving, drv, lsem.at[1])
    load_den = pltpu.make_async_copy(denominator, den, lsem.at[2])
    load_own.start()
    load_ladder(0).start()
    load_cross(0).start()
    load_drv.start()
    load_den.start()

    barrier = pltpu.get_barrier_semaphore()
    partners = [(row_dev(i), c) for i in range(7)] + [sibling, above, below, beside]
    for device in partners:
        pl.semaphore_signal(barrier, inc=1, device_id=device, device_id_type=MESH)
    load_own.wait()
    gath[r, 0:rows, :] = own[...]
    gath[r, rows:PAD, :] = jnp.zeros((PAD - rows, width), F32)
    pl.semaphore_wait(barrier, len(partners))

    def hop(i, shard, device, columns=None):
        ref = gath.at[shard] if columns is None else gath.at[shard, :, pl.ds(columns, half)]
        return remote(ref, ref, gs.at[i], gr.at[i], device)

    g1, g2, g3 = hop(0, r, right), hop(1, r, left), hop(2, r, across)
    g1.start()
    g2.start()
    g3.start()
    tables(rows, channel_slot, channel_of, source_row, target_row, recoupling, meta, tgt)
    mcopies = []
    for i in range(7):
        copy = remote(meta.at[row_dev(i)], mrecv.at[r], ms.at[i], mr.at[i], (row_dev(i), c))
        copy.start()
        mcopies.append(copy)
    tcopy = remote(tgt, tsib, ms.at[7], mr.at[7], sibling)
    tcopy.start()
    mrecv[r] = meta[r]

    @pl.loop(0, 2 * chunks)
    def _(p):
        load_ladder(p).wait()

        @pl.when(p + 1 < 2 * chunks)
        def _():
            load_ladder(p + 1).start()

        high, low = split(stage[p % 2])
        chi[p] = high
        clo[p] = low

    slots = NROW * CAP
    pairs = [
        (r, x * 2 + 1 - yh),
        (xm1 * 2 + yh, xp * 2 + yh),
        (x2 * 2 + yh, xm1 * 2 + 1 - yh),
        (xp * 2 + 1 - yh, x2 * 2 + 1 - yh),
    ]
    units = [shard for pair in pairs for shard in pair]
    group = 2 * PAD

    def place(g, shape, axis):
        index = lax.broadcasted_iota(jnp.int32, shape, axis)
        return jnp.where(index < PAD, index + pairs[g][0] * PAD, index + (pairs[g][1] - 1) * PAD).astype(F32)

    def convert(g):
        high, low = split(jnp.concatenate([gath[pairs[g][0]], gath[pairs[g][1]]], axis=0))
        ahi[g] = high
        alo[g] = low

    def take(g):
        chosen = jnp.where(place(g, (slots, group), 1) == colb[:, 0:1], 1.0, 0.0).astype(BF16)
        for n in range(chunks):
            columns = slice(n * CHUNK, (n + 1) * CHUNK)
            part = dot(chosen, ahi[g, :, columns]) + dot(chosen, alo[g, :, columns])
            if g == 0:
                pacc[:, columns] = part
            else:
                pacc[:, columns] += part

    def ladder(s, k, target, h):
        p = s * chunks + k
        high = ahi[2 * h : 2 * h + 2].reshape(2 * group, width)
        low = alo[2 * h : 2 * h + 2].reshape(2 * group, width)
        value = dot_t(high, chi[p]) + dot_t(low, chi[p]) + dot_t(high, clo[p])
        for i in range(4):
            target[units[4 * h + i]] = value[i * PAD : (i + 1) * PAD]

    def both(k, h):
        ladder(1 - core, k, sib.at[k], h)
        ladder(core, k, mine.at[k], h)

    n_left, n_right, n_across, n_far = xm1 * 2 + yh, xp * 2 + yh, x * 2 + 1 - yh, x2 * 2 + yh
    hop(0, n_left, right).wait_recv()
    g4 = hop(3, n_left, right, 0)
    g4.start()
    hop(1, n_right, left).wait_recv()
    g5 = hop(4, n_right, left, half)
    g5.start()
    convert(1)
    hop(2, n_across, across).wait_recv()
    convert(0)

    @pl.loop(0, 2)
    def _(k):
        both(k, 0)

    g4.wait_send()
    g5.wait_send()
    g6, g7 = hop(5, n_across, right), hop(6, n_across, left)
    g6.start()
    g7.start()
    hop(3, n_far, right, 0).wait_recv()
    hop(4, n_far, left, half).wait_recv()
    g8 = hop(7, n_far, across)
    g8.start()

    @pl.loop(2, chunks)
    def _(k):
        both(k, 0)

    @pl.loop(0, chunks)
    def _(p):
        load_cross(p).wait()

        @pl.when(p + 1 < chunks)
        def _():
            load_cross(p + 1).start()

        high, low = split(xstage[p % 2])
        xhi[p] = high
        xlo[p] = low

    for i in range(7):
        remote(meta.at[r], mrecv.at[row_src(i)], ms.at[i], mr.at[i], (row_src(i), c)).wait_recv()
    diagonal = lax.broadcasted_iota(jnp.int32, (CAP, 128), 0) == lax.broadcasted_iota(jnp.int32, (CAP, 128), 1)
    for s in range(NROW):
        for row, target in ((0, colb), (1, colc)):
            column = jnp.sum(jnp.where(diagonal, mrecv[s, row : row + 1, :], 0.0), axis=1, keepdims=True)
            target[s * CAP : (s + 1) * CAP, :] = jnp.broadcast_to(column, (CAP, 128))
    take(0)
    take(1)
    tcopy.wait_recv()
    tall[:, 0:slots] = tgt[pl.ds(core, 1), :]
    tall[:, slots : 2 * slots] = tsib[pl.ds(core, 1), :]
    for g in range(4):
        hit = jnp.where(place(g, (group, 2 * slots), 0) == tall[...], 1.0, 0.0)
        onehot[g] = hit.astype(BF16)

    hop(5, xm1 * 2 + 1 - yh, right).wait_recv()
    convert(2)
    take(2)
    hop(6, xp * 2 + 1 - yh, left).wait_recv()
    hop(7, x2 * 2 + 1 - yh, across).wait_recv()
    convert(3)
    take(3)
    for n in range(chunks):
        columns = slice(n * CHUNK, (n + 1) * CHUNK)
        high, low = split(pacc[:, columns] * colc[:, 0:1])
        phi[:, columns] = high
        plo[:, columns] = low

    def returned(k, i, source):
        return remote(cross.at[k, source], back.at[k, r], ts.at[k, i], tr.at[k, i], (source, c))

    def product(k):
        value = dot(phi[...], xhi[k]) + dot(plo[...], xhi[k]) + dot(phi[...], xlo[k])
        cross[k] = value.reshape(NROW, CAP, CHUNK)
        for i in range(7):
            returned(k, i, row_dev(i)).start()
        back[k, r] = cross[k, r]

    def scatter(k):
        high, low = split(jnp.concatenate([back[k].reshape(slots, CHUNK), bsib[k].reshape(slots, CHUNK)], axis=0))
        hits = onehot[...].reshape(4 * group, 2 * slots)
        value = dot(hits, high) + dot(hits, low)
        for i in range(8):
            mine[k, units[i]] += value[i * PAD : (i + 1) * PAD] + crecv[k, units[i]]

    def to_sibling(k):
        return remote(sib.at[k], crecv.at[k], cs.at[k], cr.at[k], sibling)

    def unit(k, depth, side):
        return mine.at[k, side * 4 + depth]

    def pass_on(k):
        return remote(back.at[k], bsib.at[k], bs.at[k], br.at[k], sibling)

    def around(k, i):
        source, device = [
            (unit(k, z2, 0), above),
            (unit(k, z2, 1), below),
            (unit(k, zp, 1), above),
            (unit(k, zm, 0), below),
            (unit(k, zp, 0), above),
            (unit(k, zm, 1), below),
        ][i]
        return remote(source, zrecv.at[k, i], zs.at[k, i], zr.at[k, i], device)

    quarter = CHUNK // 2
    same, other = yl * 4, (1 - yl) * 4

    def far_around(k, i):
        source, target, device = [
            (unit(k, zp, 1 - yl), zrecv.at[k, 0], above),
            (unit(k, zm, 1 - yl), zrecv.at[k, 1], below),
            (unit(k, z2, yl).at[:, 0:quarter], zrecv.at[k, 2, :, 0:quarter], above),
            (unit(k, z2, yl).at[:, quarter:CHUNK], zrecv.at[k, 3, :, quarter:CHUNK], below),
            (unit(k, zp, yl), zrecv.at[k, 4], above),
            (unit(k, zm, yl), zrecv.at[k, 5], below),
        ][i]
        return remote(source, target, zs.at[k, i], zr.at[k, i], device)

    def aside(k, i):
        return remote(unit(k, z if i else z2, 1 - yl), yrecv.at[k, i], ys.at[k, i], yr.at[k, i], beside)

    def exchange(k):
        return remote(esend.at[k], erecv.at[k], es.at[k], er.at[k], sibling)

    def solve(k, half_index, value):
        columns = pl.ds(pl.multiple_of(half_index * width + k * CHUNK, CHUNK), CHUNK)
        out[:, columns] = (drv[:, columns] + value) / den[:, columns]

    def late(k):
        ladder(1 - core, k, sib.at[k], 1)
        to_sibling(k).start()
        ladder(core, k, mine.at[k], 1)

    product(0)
    product(1)
    late(0)
    load_drv.wait()
    load_den.wait()
    block = rows // 2
    final = yl * 4 + z

    @pl.loop(0, chunks + 4)
    def _(t):
        @pl.when(t < chunks)
        def _():
            for i in range(7):
                remote(
                    cross.at[t, r], back.at[t, row_src(i)], ts.at[t, i], tr.at[t, i], (row_src(i), c)
                ).wait_recv()
            pass_on(t).start()

            @pl.when(t + 2 < chunks)
            def _():
                product(t + 2)

        @pl.when(t + 1 < chunks)
        def _():
            late(t + 1)

        @pl.when((t >= FAR + 1) & (t < chunks + 1))
        def _():
            k = t - 1
            aside(k, 0).wait_recv()
            mine[k, same + z2] += yrecv[k, 0]
            far_around(k, 2).start()
            far_around(k, 3).start()

        @pl.when(t < chunks)
        def _():
            to_sibling(t).wait_recv()
            pass_on(t).wait_recv()
            scatter(t)

        @pl.when(t < FAR)
        def _():
            for i in range(4):
                around(t, i).start()

        @pl.when((t >= FAR) & (t < chunks))
        def _():
            aside(t, 0).start()
            far_around(t, 0).start()
            far_around(t, 1).start()

        @pl.when((t >= FAR + 1) & (t < chunks + 1))
        def _():
            k = t - 1
            far_around(k, 0).wait_recv()
            far_around(k, 1).wait_recv()
            mine[k, other + z] += zrecv[k, 0] + zrecv[k, 1]
            aside(k, 1).start()
            far_around(k, 2).wait_recv()
            mine[k, same + zp, :, 0:quarter] += zrecv[k, 2, :, 0:quarter]
            far_around(k, 4).start()
            far_around(k, 3).wait_recv()
            mine[k, same + zm, :, quarter:CHUNK] += zrecv[k, 3, :, quarter:CHUNK]
            far_around(k, 5).start()

        @pl.when((t >= 1) & (t < FAR + 1))
        def _():
            k = t - 1
            around(k, 0).wait_recv()
            mine[k, zp] += zrecv[k, 0]
            around(k, 4).start()
            around(k, 1).wait_recv()
            mine[k, 4 + zm] += zrecv[k, 1]
            around(k, 5).start()

        @pl.when((t >= 2) & (t < FAR + 2))
        def _():
            k = t - 2
            for i in range(2, 6):
                around(k, i).wait_recv()
            mine[k, z] += zrecv[k, 3] + zrecv[k, 4]
            mine[k, 4 + z] += zrecv[k, 2] + zrecv[k, 5]
            aside(k, 1).start()

        @pl.when((t >= 3) & (t < chunks + 3))
        def _():
            k = t - 3

            @pl.when(k >= FAR)
            def _():
                far_around(k, 4).wait_recv()
                far_around(k, 5).wait_recv()
                mine[k, final] += zrecv[k, 4] + zrecv[k, 5]

            aside(k, 1).wait_recv()
            mine[k, final] += yrecv[k, 1]
            low = mine[k, final, 0:block, :]
            high = mine[k, final, block:rows, :]
            esend[k] = jnp.where(core == 0, high, low)
            exchange(k).start()
            solve(k, core, jnp.where(core == 0, low, high))

        @pl.when(t >= 4)
        def _():
            k = t - 4
            exchange(k).wait_recv()
            solve(k, 1 - core, erecv[k])

    for copy in [g1, g2, g3, g6, g7, g8, tcopy] + mcopies:
        copy.wait_send()

    @pl.loop(0, chunks)
    def _(k):
        for i in range(7):
            returned(k, i, row_dev(i)).wait_send()
        to_sibling(k).wait_send()
        aside(k, 1).wait_send()
        pass_on(k).wait_send()
        exchange(k).wait_send()

    @pl.loop(0, FAR)
    def _(k):
        for i in range(6):
            around(k, i).wait_send()

    @pl.loop(FAR, chunks)
    def _(k):
        for i in range(6):
            far_around(k, i).wait_send()
        aside(k, 0).wait_send()


def tables(shard, channel_slot, channel_of, source_row, target_row, recoupling, meta, tgt):
    items = channel_of.shape[1]
    channel = channel_of[...]
    owner = jnp.zeros(channel.shape, jnp.int32)
    for i in range(NROW):
        owner = jnp.where(channel == i, channel_slot[i], owner)
    marks = jnp.where(lax.broadcasted_iota(jnp.int32, (NROW, items), 0) == owner, 1.0, 0.0)
    square = (items, items)
    down, along = lax.broadcasted_iota(jnp.int32, square, 0), lax.broadcasted_iota(jnp.int32, square, 1)
    before = dot(marks.astype(BF16), jnp.where(down < along, 1.0, 0.0).astype(BF16))
    slot = owner.astype(F32) * CAP + jnp.sum(marks * before, axis=0, keepdims=True)

    def padded(row):
        passed = row
        for i in range(1, NROW):
            passed = passed + jnp.where(row >= i * shard, PAD - shard, 0)
        return passed.astype(F32)

    def column(row):
        return jnp.sum(jnp.where(down == along, row, 0.0), axis=1, keepdims=True)

    target = target_row[...]
    slot_c, scale_c = column(slot), column(recoupling[...])
    source_c, hole_c = column(padded(source_row[...])), column(padded(target >> 1))
    odd_c = column((target & 1).astype(F32))
    lanes = along.astype(F32)
    for i in range(NROW):
        match = slot_c == lanes + i * CAP
        meta[i, 0:1, :] = jnp.sum(jnp.where(match, source_c + 1.0, 0.0), axis=0, keepdims=True) - 1.0
        meta[i, 1:2, :] = jnp.sum(jnp.where(match, scale_c, 0.0), axis=0, keepdims=True)
        meta[i, 2:8, :] = jnp.zeros((6, items), F32)
    slots = NROW * CAP
    match = slot_c == lax.broadcasted_iota(jnp.int32, (items, slots), 1).astype(F32)
    for i in range(2):
        hit = match & (odd_c == float(i))
        tgt[i : i + 1, :] = jnp.sum(jnp.where(hit, hole_c + 1.0, 0.0), axis=0, keepdims=True) - 1.0


def on_device(
    amplitude,
    ladder_coupling,
    crossed_coupling,
    channel_slot,
    channel_of,
    source_row,
    target_row,
    recoupling,
    driving,
    denominator,
):
    rows, width = amplitude.shape
    chunks = width // CHUNK
    slots = NROW * CAP
    group = 2 * PAD
    dma = pltpu.SemaphoreType.DMA
    vmem = pltpu.VMEM
    return pl.pallas_call(
        kernel,
        out_shape=jax.ShapeDtypeStruct((rows // 2, 2 * width), F32),
        in_specs=[pl.BlockSpec(memory_space=pltpu.SMEM)]
        + [pl.BlockSpec(memory_space=pltpu.VMEM)] * 4
        + [pl.BlockSpec(memory_space=pl.ANY)] * 5,
        out_specs=pl.BlockSpec(memory_space=pltpu.VMEM),
        scratch_shapes=[
            vmem((rows, width), F32),
            vmem((NROW, PAD, width), F32),
            vmem((4, group, width), BF16),
            vmem((4, group, width), BF16),
            vmem((2, CHUNK, width), F32),
            vmem((2 * chunks, CHUNK, width), BF16),
            vmem((2 * chunks, CHUNK, width), BF16),
            vmem((2, width, CHUNK), F32),
            vmem((chunks, width, CHUNK), BF16),
            vmem((chunks, width, CHUNK), BF16),
            vmem((NROW, 8, 128), F32),
            vmem((NROW, 8, 128), F32),
            vmem((2, slots), F32),
            vmem((2, slots), F32),
            vmem((1, 2 * slots), F32),
            vmem((slots, 128), F32),
            vmem((slots, 128), F32),
            vmem((slots, width), F32),
            vmem((slots, width), BF16),
            vmem((slots, width), BF16),
            vmem((4, group, 2 * slots), BF16),
            vmem((chunks, NROW, CAP, CHUNK), F32),
            vmem((chunks, NROW, CAP, CHUNK), F32),
            vmem((chunks, NROW, CAP, CHUNK), F32),
            vmem((chunks, NROW, PAD, CHUNK), F32),
            vmem((chunks, NROW, PAD, CHUNK), F32),
            vmem((chunks, NROW, PAD, CHUNK), F32),
            vmem((chunks, 6, PAD, CHUNK), F32),
            vmem((chunks, 2, PAD, CHUNK), F32),
            vmem((chunks, rows // 2, CHUNK), F32),
            vmem((chunks, rows // 2, CHUNK), F32),
            vmem((rows // 2, 2 * width), F32),
            vmem((rows // 2, 2 * width), F32),
            dma((3,)),
            dma((4,)),
            dma((8,)),
            dma((8,)),
            dma((8,)),
            dma((8,)),
            dma((chunks, 7)),
            dma((chunks, 7)),
            dma((chunks,)),
            dma((chunks,)),
            dma((chunks,)),
            dma((chunks,)),
            dma((chunks, 6)),
            dma((chunks, 6)),
            dma((chunks, 2)),
            dma((chunks, 2)),
            dma((chunks,)),
            dma((chunks,)),
        ],
        compiler_params=pltpu.CompilerParams(
            collective_id=0, has_side_effects=True, vmem_limit_bytes=63 * 1024 * 1024
        ),
        cost_estimate=pl.CostEstimate(flops=24_000_000_000, bytes_accessed=22_000_000, transcendentals=0),
    )(
        channel_slot,
        channel_of.reshape(1, -1),
        source_row,
        target_row,
        recoupling,
        amplitude,
        ladder_coupling,
        crossed_coupling,
        driving,
        denominator,
    )


def solution(mesh):
    in_specs = (
        P("row", "col"),
        P("row", "col"),
        P("row", None, None),
        P(),
        P("col", "row", None),
        P("col", "row"),
        P("col", "row"),
        P("col", "row"),
        P("col", "row"),
        P("col", "row"),
    )
    out_specs = P("col", "row")
    return jax.shard_map(
        on_device, mesh=mesh, in_specs=in_specs, out_specs=out_specs, check_vma=False
    )
```

```python
import jax
import jax.numpy as jnp
from jax import lax
from jax.experimental import pallas as pl
from jax.experimental.pallas import tpu as pltpu
from jax.sharding import PartitionSpec as P

CAP = 40
NROW = 8
FAR = 3
PAD = 104
CHUNK = 256
MESH = pl.DeviceIdType.MESH
F32 = jnp.float32
BF16 = jnp.bfloat16
OFFSETS = [(dx, dy) for dx in (1, 3, 2, 0) for dy in (0, 1) if (dx, dy) != (0, 0)]


def split(value):
    high = value.astype(BF16)
    return high, (value - high.astype(F32)).astype(BF16)


def dot(a, b):
    return lax.dot_general(a, b, (((1,), (0,)), ((), ())), preferred_element_type=F32)


def dot_t(a, b):
    return lax.dot_general(a, b, (((1,), (1,)), ((), ())), preferred_element_type=F32)


def kernel(
    channel_slot, channel_of, source_row, target_row, recoupling, amp, lad, xm, driving, denominator, out,
    own, gath, ahi, alo, stage, chi, clo, xstage, xhi, xlo, meta, mrecv, tgt, tsib, tall, colb, colc, pacc, phi, plo,
    onehot, cross, back, bsib, sib, mine, crecv, zrecv, yrecv, esend, erecv, drv, den,
    lsem, stsem, gs, gr, ms, mr, ts, tr, bs, br, cs, cr, zs, zr, ys, yr, es, er,
):
    rows, width = amp.shape
    chunks = width // CHUNK
    half = width // 2
    r, c = lax.axis_index("row"), lax.axis_index("col")
    x, yh = r // 2, r % 2
    yl, z, core = c // 8, (c // 2) % 4, c % 2
    xp, xm1, x2 = (x + 1) % 4, (x + 3) % 4, (x + 2) % 4
    zp, zm, z2 = (z + 1) % 4, (z + 3) % 4, (z + 2) % 4

    def row_dev(i):
        dx, dy = OFFSETS[i]
        return ((x + dx) % 4) * 2 + (yh + dy) % 2

    def row_src(i):
        dx, dy = OFFSETS[i]
        return ((x + 4 - dx) % 4) * 2 + (yh + dy) % 2

    sibling = (r, yl * 8 + z * 2 + (1 - core))
    above = (r, yl * 8 + zp * 2 + core)
    below = (r, yl * 8 + zm * 2 + core)
    beside = (r, (1 - yl) * 8 + z * 2 + core)
    right, left, across = (xp * 2 + yh, c), (xm1 * 2 + yh, c), (x * 2 + 1 - yh, c)

    def remote(src, dst, send, recv, device):
        return pltpu.make_async_remote_copy(
            src_ref=src, dst_ref=dst, send_sem=send, recv_sem=recv, device_id=device, device_id_type=MESH
        )

    def load_ladder(p):
        first = (p // 2 + ((p + 1 + core) % 2) * chunks) * CHUNK
        return pltpu.make_async_copy(
            lad.at[pl.ds(pl.multiple_of(first, CHUNK), CHUNK), :], stage.at[p % 2], stsem.at[p % 2]
        )

    def load_cross(p):
        return pltpu.make_async_copy(
            xm.at[0, :, pl.ds(pl.multiple_of(p * CHUNK, CHUNK), CHUNK)], xstage.at[p % 2], stsem.at[2 + p % 2]
        )

    load_own = pltpu.make_async_copy(amp, own, lsem.at[0])
    load_drv = pltpu.make_async_copy(driving, drv, lsem.at[1])
    load_den = pltpu.make_async_copy(denominator, den, lsem.at[2])
    load_own.start()
    load_ladder(0).start()
    load_cross(0).start()
    load_drv.start()
    load_den.start()

    barrier = pltpu.get_barrier_semaphore()
    partners = [(row_dev(i), c) for i in range(7)] + [sibling, above, below, beside]
    for device in partners:
        pl.semaphore_signal(barrier, inc=1, device_id=device, device_id_type=MESH)
    load_own.wait()
    gath[r, 0:rows, :] = own[...]
    gath[r, rows:PAD, :] = jnp.zeros((PAD - rows, width), F32)
    pl.semaphore_wait(barrier, len(partners))

    def hop(i, shard, device, columns=None):
        ref = gath.at[shard] if columns is None else gath.at[shard, :, pl.ds(columns, half)]
        return remote(ref, ref, gs.at[i], gr.at[i], device)

    n_left, n_right, n_across, n_far = xm1 * 2 + yh, xp * 2 + yh, x * 2 + 1 - yh, x2 * 2 + yh
    sends = [hop(0, r, right, 0), hop(1, r, left, half), hop(2, r, across, 0)]
    sends += [hop(3, r, right, half), hop(4, r, left, 0), hop(5, r, across, half)]
    for copy in sends:
        copy.start()
    tables(rows, channel_slot, channel_of, source_row, target_row, recoupling, meta, tgt)
    mcopies = []
    for i in range(7):
        copy = remote(meta.at[row_dev(i)], mrecv.at[r], ms.at[i], mr.at[i], (row_dev(i), c))
        copy.start()
        mcopies.append(copy)
    tcopy = remote(tgt, tsib, ms.at[7], mr.at[7], sibling)
    tcopy.start()
    mrecv[r] = meta[r]

    def ladder_split(p):
        load_ladder(p).wait()

        @pl.when(p + 1 < 2 * chunks)
        def _():
            load_ladder(p + 1).start()

        high, low = split(stage[p % 2])
        chi[p] = high
        clo[p] = low

    @pl.loop(0, chunks)
    def _(p):
        ladder_split(p)

    hop(0, n_left, right, 0).wait_recv()
    g4 = hop(6, n_left, right, 0)
    g4.start()
    hop(1, n_right, left, half).wait_recv()
    g5 = hop(7, n_right, left, half)
    g5.start()

    @pl.loop(chunks, 2 * chunks)
    def _(p):
        ladder_split(p)

    slots = NROW * CAP
    pairs = [
        (r, x * 2 + 1 - yh),
        (xm1 * 2 + yh, xp * 2 + yh),
        (x2 * 2 + yh, xm1 * 2 + 1 - yh),
        (xp * 2 + 1 - yh, x2 * 2 + 1 - yh),
    ]
    units = [shard for pair in pairs for shard in pair]
    group = 2 * PAD

    def place(g, shape, axis):
        index = lax.broadcasted_iota(jnp.int32, shape, axis)
        return jnp.where(index < PAD, index + pairs[g][0] * PAD, index + (pairs[g][1] - 1) * PAD).astype(F32)

    def convert(g):
        high, low = split(jnp.concatenate([gath[pairs[g][0]], gath[pairs[g][1]]], axis=0))
        ahi[g] = high
        alo[g] = low

    def take(g):
        chosen = jnp.where(place(g, (slots, group), 1) == colb[:, 0:1], 1.0, 0.0).astype(BF16)
        for n in range(chunks):
            columns = slice(n * CHUNK, (n + 1) * CHUNK)
            part = dot(chosen, ahi[g, :, columns]) + dot(chosen, alo[g, :, columns])
            if g == 0:
                pacc[:, columns] = part
            else:
                pacc[:, columns] += part

    def both(k, h):
        high = ahi[2 * h : 2 * h + 2].reshape(2 * group, width)
        low = alo[2 * h : 2 * h + 2].reshape(2 * group, width)
        chigh = chi[pl.ds(2 * k, 2)].reshape(2 * CHUNK, width)
        clow = clo[pl.ds(2 * k, 2)].reshape(2 * CHUNK, width)
        value = dot_t(high, chigh) + dot_t(low, chigh) + dot_t(high, clow)
        for i in range(4):
            sib[k, units[4 * h + i]] = value[i * PAD : (i + 1) * PAD, 0:CHUNK]
            mine[k, units[4 * h + i]] = value[i * PAD : (i + 1) * PAD, CHUNK : 2 * CHUNK]

    @pl.loop(0, chunks)
    def _(p):
        load_cross(p).wait()

        @pl.when(p + 1 < chunks)
        def _():
            load_cross(p + 1).start()

        high, low = split(xstage[p % 2])
        xhi[p] = high
        xlo[p] = low

    for i in range(7):
        remote(meta.at[r], mrecv.at[row_src(i)], ms.at[i], mr.at[i], (row_src(i), c)).wait_recv()
    diagonal = lax.broadcasted_iota(jnp.int32, (CAP, 128), 0) == lax.broadcasted_iota(jnp.int32, (CAP, 128), 1)
    for s in range(NROW):
        for row, target in ((0, colb), (1, colc)):
            column = jnp.sum(jnp.where(diagonal, mrecv[s, row : row + 1, :], 0.0), axis=1, keepdims=True)
            target[s * CAP : (s + 1) * CAP, :] = jnp.broadcast_to(column, (CAP, 128))
    tcopy.wait_recv()
    tall[:, 0:slots] = tgt[pl.ds(core, 1), :]
    tall[:, slots : 2 * slots] = tsib[pl.ds(core, 1), :]
    for g in range(4):
        hit = jnp.where(place(g, (group, 2 * slots), 0) == tall[...], 1.0, 0.0)
        onehot[g, :, 0 : 2 * slots] = hit.astype(BF16)
        onehot[g, :, 2 * slots : 4 * slots] = hit.astype(BF16)

    hop(2, n_across, across, 0).wait_recv()
    hop(5, n_across, across, half).wait_recv()
    convert(0)
    g4.wait_send()
    g5.wait_send()
    g6, g7 = hop(8, n_across, right), hop(9, n_across, left)
    g6.start()
    g7.start()
    hop(6, n_far, right, 0).wait_recv()
    g8 = hop(10, n_far, across, 0)
    g8.start()
    hop(7, n_far, left, half).wait_recv()
    g9 = hop(11, n_far, across, half)
    g9.start()
    hop(3, n_left, right, half).wait_recv()
    hop(4, n_right, left, 0).wait_recv()
    convert(1)

    @pl.loop(0, chunks)
    def _(k):
        both(k, 0)

    take(0)
    take(1)
    hop(8, xm1 * 2 + 1 - yh, right).wait_recv()
    convert(2)
    take(2)
    hop(9, xp * 2 + 1 - yh, left).wait_recv()
    hop(10, x2 * 2 + 1 - yh, across, 0).wait_recv()
    hop(11, x2 * 2 + 1 - yh, across, half).wait_recv()
    convert(3)
    take(3)
    for n in range(chunks):
        columns = slice(n * CHUNK, (n + 1) * CHUNK)
        high, low = split(pacc[:, columns] * colc[:, 0:1])
        phi[:, columns] = high
        plo[:, columns] = low

    def returned(k, i, source):
        return remote(cross.at[k, source], back.at[k, r], ts.at[k, i], tr.at[k, i], (source, c))

    def product(k):
        value = dot(phi[...], xhi[k]) + dot(plo[...], xhi[k]) + dot(phi[...], xlo[k])
        cross[k] = value.reshape(NROW, CAP, CHUNK)
        for i in range(7):
            returned(k, i, row_dev(i)).start()
        back[k, r] = cross[k, r]

    def scatter(k):
        high, low = split(jnp.concatenate([back[k].reshape(slots, CHUNK), bsib[k].reshape(slots, CHUNK)], axis=0))
        value = dot(onehot[...].reshape(4 * group, 4 * slots), jnp.concatenate([high, low], axis=0))
        for i in range(8):
            mine[k, units[i]] += value[i * PAD : (i + 1) * PAD] + crecv[k, units[i]]

    def to_sibling(k):
        return remote(sib.at[k], crecv.at[k], cs.at[k], cr.at[k], sibling)

    def unit(k, depth, side):
        return mine.at[k, side * 4 + depth]

    def pass_on(k):
        return remote(back.at[k], bsib.at[k], bs.at[k], br.at[k], sibling)

    def around(k, i):
        source, device = [
            (unit(k, z2, 0), above),
            (unit(k, z2, 1), below),
            (unit(k, zp, 1), above),
            (unit(k, zm, 0), below),
            (unit(k, zp, 0), above),
            (unit(k, zm, 1), below),
        ][i]
        return remote(source, zrecv.at[k, i], zs.at[k, i], zr.at[k, i], device)

    quarter = CHUNK // 2
    same, other = yl * 4, (1 - yl) * 4

    def far_around(k, i):
        source, target, device = [
            (unit(k, zp, 1 - yl), zrecv.at[k, 0], above),
            (unit(k, zm, 1 - yl), zrecv.at[k, 1], below),
            (unit(k, z2, yl).at[:, 0:quarter], zrecv.at[k, 2, :, 0:quarter], above),
            (unit(k, z2, yl).at[:, quarter:CHUNK], zrecv.at[k, 3, :, quarter:CHUNK], below),
            (unit(k, zp, yl), zrecv.at[k, 4], above),
            (unit(k, zm, yl), zrecv.at[k, 5], below),
        ][i]
        return remote(source, target, zs.at[k, i], zr.at[k, i], device)

    def aside(k, i):
        return remote(unit(k, z if i else z2, 1 - yl), yrecv.at[k, i], ys.at[k, i], yr.at[k, i], beside)

    def exchange(k):
        return remote(esend.at[k], erecv.at[k], es.at[k], er.at[k], sibling)

    def solve(k, half_index, value):
        columns = pl.ds(pl.multiple_of(half_index * width + k * CHUNK, CHUNK), CHUNK)
        out[:, columns] = (drv[:, columns] + value) / den[:, columns]

    def late(k):
        both(k, 1)
        to_sibling(k).start()

    product(0)
    product(1)
    late(0)
    load_drv.wait()
    load_den.wait()
    block = rows // 2
    final = yl * 4 + z

    @pl.loop(0, chunks + 4)
    def _(t):
        @pl.when(t < chunks)
        def _():
            for i in range(7):
                remote(
                    cross.at[t, r], back.at[t, row_src(i)], ts.at[t, i], tr.at[t, i], (row_src(i), c)
                ).wait_recv()
            pass_on(t).start()

            @pl.when(t + 2 < chunks)
            def _():
                product(t + 2)

        @pl.when(t + 1 < chunks)
        def _():
            late(t + 1)

        @pl.when((t >= FAR + 1) & (t < chunks + 1))
        def _():
            k = t - 1
            aside(k, 0).wait_recv()
            mine[k, same + z2] += yrecv[k, 0]
            far_around(k, 2).start()
            far_around(k, 3).start()

        @pl.when(t < chunks)
        def _():
            to_sibling(t).wait_recv()
            pass_on(t).wait_recv()
            scatter(t)

        @pl.when(t < FAR)
        def _():
            for i in range(4):
                around(t, i).start()

        @pl.when((t >= FAR) & (t < chunks))
        def _():
            aside(t, 0).start()
            far_around(t, 0).start()
            far_around(t, 1).start()

        @pl.when((t >= FAR + 1) & (t < chunks + 1))
        def _():
            k = t - 1
            far_around(k, 0).wait_recv()
            far_around(k, 1).wait_recv()
            mine[k, other + z] += zrecv[k, 0] + zrecv[k, 1]
            aside(k, 1).start()
            far_around(k, 2).wait_recv()
            mine[k, same + zp, :, 0:quarter] += zrecv[k, 2, :, 0:quarter]
            far_around(k, 4).start()
            far_around(k, 3).wait_recv()
            mine[k, same + zm, :, quarter:CHUNK] += zrecv[k, 3, :, quarter:CHUNK]
            far_around(k, 5).start()

        @pl.when((t >= 1) & (t < FAR + 1))
        def _():
            k = t - 1
            around(k, 0).wait_recv()
            mine[k, zp] += zrecv[k, 0]
            around(k, 4).start()
            around(k, 1).wait_recv()
            mine[k, 4 + zm] += zrecv[k, 1]
            around(k, 5).start()

        @pl.when((t >= 2) & (t < FAR + 2))
        def _():
            k = t - 2
            for i in range(2, 6):
                around(k, i).wait_recv()
            mine[k, z] += zrecv[k, 3] + zrecv[k, 4]
            mine[k, 4 + z] += zrecv[k, 2] + zrecv[k, 5]
            aside(k, 1).start()

        @pl.when((t >= 3) & (t < chunks + 3))
        def _():
            k = t - 3

            @pl.when(k >= FAR)
            def _():
                far_around(k, 4).wait_recv()
                far_around(k, 5).wait_recv()
                mine[k, final] += zrecv[k, 4] + zrecv[k, 5]

            aside(k, 1).wait_recv()
            mine[k, final] += yrecv[k, 1]
            low = mine[k, final, 0:block, :]
            high = mine[k, final, block:rows, :]
            esend[k] = jnp.where(core == 0, high, low)
            exchange(k).start()
            solve(k, core, jnp.where(core == 0, low, high))

        @pl.when(t >= 4)
        def _():
            k = t - 4
            exchange(k).wait_recv()
            solve(k, 1 - core, erecv[k])

    for copy in sends + [g6, g7, g8, g9, tcopy] + mcopies:
        copy.wait_send()

    @pl.loop(0, chunks)
    def _(k):
        for i in range(7):
            returned(k, i, row_dev(i)).wait_send()
        to_sibling(k).wait_send()
        aside(k, 1).wait_send()
        pass_on(k).wait_send()
        exchange(k).wait_send()

    @pl.loop(0, FAR)
    def _(k):
        for i in range(6):
            around(k, i).wait_send()

    @pl.loop(FAR, chunks)
    def _(k):
        for i in range(6):
            far_around(k, i).wait_send()
        aside(k, 0).wait_send()


def tables(shard, channel_slot, channel_of, source_row, target_row, recoupling, meta, tgt):
    items = channel_of.shape[1]
    channel = channel_of[...]
    owner = jnp.zeros(channel.shape, jnp.int32)
    for i in range(NROW):
        owner = jnp.where(channel == i, channel_slot[i], owner)
    marks = jnp.where(lax.broadcasted_iota(jnp.int32, (NROW, items), 0) == owner, 1.0, 0.0)
    square = (items, items)
    down, along = lax.broadcasted_iota(jnp.int32, square, 0), lax.broadcasted_iota(jnp.int32, square, 1)
    before = dot(marks.astype(BF16), jnp.where(down < along, 1.0, 0.0).astype(BF16))
    slot = owner.astype(F32) * CAP + jnp.sum(marks * before, axis=0, keepdims=True)

    def padded(row):
        passed = row
        for i in range(1, NROW):
            passed = passed + jnp.where(row >= i * shard, PAD - shard, 0)
        return passed.astype(F32)

    def column(row):
        return jnp.sum(jnp.where(down == along, row, 0.0), axis=1, keepdims=True)

    target = target_row[...]
    slot_c, scale_c = column(slot), column(recoupling[...])
    source_c, hole_c = column(padded(source_row[...])), column(padded(target >> 1))
    odd_c = column((target & 1).astype(F32))
    lanes = along.astype(F32)
    for i in range(NROW):
        match = slot_c == lanes + i * CAP
        meta[i, 0:1, :] = jnp.sum(jnp.where(match, source_c + 1.0, 0.0), axis=0, keepdims=True) - 1.0
        meta[i, 1:2, :] = jnp.sum(jnp.where(match, scale_c, 0.0), axis=0, keepdims=True)
        meta[i, 2:8, :] = jnp.zeros((6, items), F32)
    slots = NROW * CAP
    match = slot_c == lax.broadcasted_iota(jnp.int32, (items, slots), 1).astype(F32)
    for i in range(2):
        hit = match & (odd_c == float(i))
        tgt[i : i + 1, :] = jnp.sum(jnp.where(hit, hole_c + 1.0, 0.0), axis=0, keepdims=True) - 1.0


def on_device(
    amplitude,
    ladder_coupling,
    crossed_coupling,
    channel_slot,
    channel_of,
    source_row,
    target_row,
    recoupling,
    driving,
    denominator,
):
    rows, width = amplitude.shape
    chunks = width // CHUNK
    slots = NROW * CAP
    group = 2 * PAD
    dma = pltpu.SemaphoreType.DMA
    vmem = pltpu.VMEM
    return pl.pallas_call(
        kernel,
        out_shape=jax.ShapeDtypeStruct((rows // 2, 2 * width), F32),
        in_specs=[pl.BlockSpec(memory_space=pltpu.SMEM)]
        + [pl.BlockSpec(memory_space=pltpu.VMEM)] * 4
        + [pl.BlockSpec(memory_space=pl.ANY)] * 5,
        out_specs=pl.BlockSpec(memory_space=pltpu.VMEM),
        scratch_shapes=[
            vmem((rows, width), F32),
            vmem((NROW, PAD, width), F32),
            vmem((4, group, width), BF16),
            vmem((4, group, width), BF16),
            vmem((2, CHUNK, width), F32),
            vmem((2 * chunks, CHUNK, width), BF16),
            vmem((2 * chunks, CHUNK, width), BF16),
            vmem((2, width, CHUNK), F32),
            vmem((chunks, width, CHUNK), BF16),
            vmem((chunks, width, CHUNK), BF16),
            vmem((NROW, 8, 128), F32),
            vmem((NROW, 8, 128), F32),
            vmem((2, slots), F32),
            vmem((2, slots), F32),
            vmem((1, 2 * slots), F32),
            vmem((slots, 128), F32),
            vmem((slots, 128), F32),
            vmem((slots, width), F32),
            vmem((slots, width), BF16),
            vmem((slots, width), BF16),
            vmem((4, group, 4 * slots), BF16),
            vmem((chunks, NROW, CAP, CHUNK), F32),
            vmem((chunks, NROW, CAP, CHUNK), F32),
            vmem((chunks, NROW, CAP, CHUNK), F32),
            vmem((chunks, NROW, PAD, CHUNK), F32),
            vmem((chunks, NROW, PAD, CHUNK), F32),
            vmem((chunks, NROW, PAD, CHUNK), F32),
            vmem((chunks, 6, PAD, CHUNK), F32),
            vmem((chunks, 2, PAD, CHUNK), F32),
            vmem((chunks, rows // 2, CHUNK), F32),
            vmem((chunks, rows // 2, CHUNK), F32),
            vmem((rows // 2, 2 * width), F32),
            vmem((rows // 2, 2 * width), F32),
            dma((3,)),
            dma((4,)),
            dma((12,)),
            dma((12,)),
            dma((8,)),
            dma((8,)),
            dma((chunks, 7)),
            dma((chunks, 7)),
            dma((chunks,)),
            dma((chunks,)),
            dma((chunks,)),
            dma((chunks,)),
            dma((chunks, 6)),
            dma((chunks, 6)),
            dma((chunks, 2)),
            dma((chunks, 2)),
            dma((chunks,)),
            dma((chunks,)),
        ],
        compiler_params=pltpu.CompilerParams(
            collective_id=0, has_side_effects=True, vmem_limit_bytes=63 * 1024 * 1024
        ),
        cost_estimate=pl.CostEstimate(flops=24_000_000_000, bytes_accessed=22_000_000, transcendentals=0),
    )(
        channel_slot,
        channel_of.reshape(1, -1),
        source_row,
        target_row,
        recoupling,
        amplitude,
        ladder_coupling,
        crossed_coupling,
        driving,
        denominator,
    )


def solution(mesh):
    in_specs = (
        P("row", "col"),
        P("row", "col"),
        P("row", None, None),
        P(),
        P("col", "row", None),
        P("col", "row"),
        P("col", "row"),
        P("col", "row"),
        P("col", "row"),
        P("col", "row"),
    )
    out_specs = P("col", "row")
    return jax.shard_map(
        on_device, mesh=mesh, in_specs=in_specs, out_specs=out_specs, check_vma=False
    )
```

```python
import jax
import jax.numpy as jnp
from jax import lax
from jax.experimental import pallas as pl
from jax.experimental.pallas import tpu as pltpu
from jax.sharding import PartitionSpec as P

CAP = 40
NROW = 8
FAR = 3
PAD = 104
CHUNK = 256
MESH = pl.DeviceIdType.MESH
F32 = jnp.float32
BF16 = jnp.bfloat16
OFFSETS = [(dx, dy) for dx in (1, 3, 2, 0) for dy in (0, 1) if (dx, dy) != (0, 0)]


def split(value):
    high = value.astype(BF16)
    return high, (value - high.astype(F32)).astype(BF16)


def dot(a, b):
    return lax.dot_general(a, b, (((1,), (0,)), ((), ())), preferred_element_type=F32)


def dot_t(a, b):
    return lax.dot_general(a, b, (((1,), (1,)), ((), ())), preferred_element_type=F32)


def kernel(
    channel_slot, channel_of, source_row, target_row, recoupling, amp, lad, xm, driving, denominator, out,
    own, gath, ahi, alo, stage, chi, clo, xstage, xhi, xlo, meta, mrecv, tgt, tsib, tall, colb, colc, pacc, phi, plo,
    onehot, cross, back, bsib, sib, mine, crecv, zrecv, yrecv, esend, erecv, drv, den,
    lsem, stsem, gs, gr, ms, mr, ts, tr, bs, br, cs, cr, zs, zr, ys, yr, es, er,
):
    rows, width = amp.shape
    chunks = width // CHUNK
    half = width // 2
    r, c = lax.axis_index("row"), lax.axis_index("col")
    x, yh = r // 2, r % 2
    yl, z, core = c // 8, (c // 2) % 4, c % 2
    xp, xm1, x2 = (x + 1) % 4, (x + 3) % 4, (x + 2) % 4
    zp, zm, z2 = (z + 1) % 4, (z + 3) % 4, (z + 2) % 4

    def row_dev(i):
        dx, dy = OFFSETS[i]
        return ((x + dx) % 4) * 2 + (yh + dy) % 2

    def row_src(i):
        dx, dy = OFFSETS[i]
        return ((x + 4 - dx) % 4) * 2 + (yh + dy) % 2

    sibling = (r, yl * 8 + z * 2 + (1 - core))
    above = (r, yl * 8 + zp * 2 + core)
    below = (r, yl * 8 + zm * 2 + core)
    beside = (r, (1 - yl) * 8 + z * 2 + core)
    right, left, across = (xp * 2 + yh, c), (xm1 * 2 + yh, c), (x * 2 + 1 - yh, c)

    def remote(src, dst, send, recv, device):
        return pltpu.make_async_remote_copy(
            src_ref=src, dst_ref=dst, send_sem=send, recv_sem=recv, device_id=device, device_id_type=MESH
        )

    def load_ladder(p):
        first = (p // 2 + ((p + 1 + core) % 2) * chunks) * CHUNK
        return pltpu.make_async_copy(
            lad.at[pl.ds(pl.multiple_of(first, CHUNK), CHUNK), :], stage.at[p % 2], stsem.at[p % 2]
        )

    def load_cross(p):
        return pltpu.make_async_copy(
            xm.at[0, :, pl.ds(pl.multiple_of(p * CHUNK, CHUNK), CHUNK)], xstage.at[p % 2], stsem.at[2 + p % 2]
        )

    load_own = pltpu.make_async_copy(amp, own, lsem.at[0])
    load_drv = pltpu.make_async_copy(driving, drv, lsem.at[1])
    load_den = pltpu.make_async_copy(denominator, den, lsem.at[2])
    load_own.start()
    load_ladder(0).start()
    load_cross(0).start()
    load_drv.start()
    load_den.start()

    barrier = pltpu.get_barrier_semaphore()
    partners = [(row_dev(i), c) for i in range(7)] + [sibling, above, below, beside]
    for device in partners:
        pl.semaphore_signal(barrier, inc=1, device_id=device, device_id_type=MESH)
    load_own.wait()
    gath[r, 0:rows, :] = own[...]
    gath[r, rows:PAD, :] = jnp.zeros((PAD - rows, width), F32)
    pl.semaphore_wait(barrier, len(partners))

    def hop(i, shard, device, columns=None):
        ref = gath.at[shard] if columns is None else gath.at[shard, :, pl.ds(columns, half)]
        return remote(ref, ref, gs.at[i], gr.at[i], device)

    n_left, n_right, n_across, n_far = xm1 * 2 + yh, xp * 2 + yh, x * 2 + 1 - yh, x2 * 2 + yh
    sends = [hop(0, r, right, 0), hop(1, r, left, half), hop(2, r, across, 0)]
    sends += [hop(3, r, right, half), hop(4, r, left, 0), hop(5, r, across, half)]
    for copy in sends:
        copy.start()
    tables(rows, channel_slot, channel_of, source_row, target_row, recoupling, meta, tgt)
    mcopies = []
    for i in range(7):
        copy = remote(meta.at[row_dev(i)], mrecv.at[r], ms.at[i], mr.at[i], (row_dev(i), c))
        copy.start()
        mcopies.append(copy)
    tcopy = remote(tgt, tsib, ms.at[7], mr.at[7], sibling)
    tcopy.start()
    mrecv[r] = meta[r]

    def ladder_split(p):
        load_ladder(p).wait()

        @pl.when(p + 1 < 2 * chunks)
        def _():
            load_ladder(p + 1).start()

        high, low = split(stage[p % 2])
        chi[p] = high
        clo[p] = low

    @pl.loop(0, chunks)
    def _(p):
        ladder_split(p)

    hop(0, n_left, right, 0).wait_recv()
    g4 = hop(6, n_left, right, 0)
    g4.start()
    hop(1, n_right, left, half).wait_recv()
    g5 = hop(7, n_right, left, half)
    g5.start()

    @pl.loop(chunks, 2 * chunks)
    def _(p):
        ladder_split(p)

    slots = NROW * CAP
    pairs = [
        (r, x * 2 + 1 - yh),
        (xm1 * 2 + yh, xp * 2 + yh),
        (x2 * 2 + yh, xm1 * 2 + 1 - yh),
        (xp * 2 + 1 - yh, x2 * 2 + 1 - yh),
    ]
    units = [shard for pair in pairs for shard in pair]
    group = 2 * PAD

    def place(g, shape, axis):
        index = lax.broadcasted_iota(jnp.int32, shape, axis)
        return jnp.where(index < PAD, index + pairs[g][0] * PAD, index + (pairs[g][1] - 1) * PAD).astype(F32)

    def convert(g):
        high, low = split(jnp.concatenate([gath[pairs[g][0]], gath[pairs[g][1]]], axis=0))
        ahi[g] = high
        alo[g] = low

    def take(g):
        chosen = jnp.where(place(g, (slots, group), 1) == colb[:, 0:1], 1.0, 0.0).astype(BF16)
        for n in range(chunks):
            columns = slice(n * CHUNK, (n + 1) * CHUNK)
            part = dot(chosen, ahi[g, :, columns]) + dot(chosen, alo[g, :, columns])
            if g == 0:
                pacc[:, columns] = part
            else:
                pacc[:, columns] += part

    def both(k, h):
        high = ahi[2 * h : 2 * h + 2].reshape(2 * group, width)
        low = alo[2 * h : 2 * h + 2].reshape(2 * group, width)
        chigh = chi[pl.ds(2 * k, 2)].reshape(2 * CHUNK, width)
        clow = clo[pl.ds(2 * k, 2)].reshape(2 * CHUNK, width)
        value = dot_t(high, chigh) + dot_t(low, chigh) + dot_t(high, clow)
        for i in range(4):
            sib[k, units[4 * h + i]] = value[i * PAD : (i + 1) * PAD, 0:CHUNK]
            mine[k, units[4 * h + i]] = value[i * PAD : (i + 1) * PAD, CHUNK : 2 * CHUNK]

    @pl.loop(0, chunks)
    def _(p):
        load_cross(p).wait()

        @pl.when(p + 1 < chunks)
        def _():
            load_cross(p + 1).start()

        high, low = split(xstage[p % 2])
        xhi[p] = high
        xlo[p] = low

    for i in range(7):
        remote(meta.at[r], mrecv.at[row_src(i)], ms.at[i], mr.at[i], (row_src(i), c)).wait_recv()
    diagonal = lax.broadcasted_iota(jnp.int32, (CAP, 128), 0) == lax.broadcasted_iota(jnp.int32, (CAP, 128), 1)
    for s in range(NROW):
        for row, target in ((0, colb), (1, colc)):
            column = jnp.sum(jnp.where(diagonal, mrecv[s, row : row + 1, :], 0.0), axis=1, keepdims=True)
            target[s * CAP : (s + 1) * CAP, :] = jnp.broadcast_to(column, (CAP, 128))
    tcopy.wait_recv()
    tall[:, 0:slots] = tgt[pl.ds(core, 1), :]
    tall[:, slots : 2 * slots] = tsib[pl.ds(core, 1), :]
    for g in range(4):
        hit = jnp.where(place(g, (group, 2 * slots), 0) == tall[...], 1.0, 0.0)
        onehot[g, :, 0 : 2 * slots] = hit.astype(BF16)
        onehot[g, :, 2 * slots : 4 * slots] = hit.astype(BF16)

    hop(2, n_across, across, 0).wait_recv()
    hop(5, n_across, across, half).wait_recv()
    convert(0)
    g4.wait_send()
    g5.wait_send()
    g6, g7 = hop(8, n_across, right), hop(9, n_across, left)
    g6.start()
    g7.start()
    hop(6, n_far, right, 0).wait_recv()
    g8 = hop(10, n_far, across, 0)
    g8.start()
    hop(7, n_far, left, half).wait_recv()
    g9 = hop(11, n_far, across, half)
    g9.start()
    hop(3, n_left, right, half).wait_recv()
    hop(4, n_right, left, 0).wait_recv()
    convert(1)

    @pl.loop(0, chunks)
    def _(k):
        both(k, 0)

    take(0)
    take(1)
    hop(8, xm1 * 2 + 1 - yh, right).wait_recv()
    convert(2)
    take(2)
    hop(9, xp * 2 + 1 - yh, left).wait_recv()
    hop(10, x2 * 2 + 1 - yh, across, 0).wait_recv()
    hop(11, x2 * 2 + 1 - yh, across, half).wait_recv()
    convert(3)
    take(3)
    for n in range(chunks):
        columns = slice(n * CHUNK, (n + 1) * CHUNK)
        high, low = split(pacc[:, columns] * colc[:, 0:1])
        phi[:, columns] = high
        plo[:, columns] = low

    def returned(k, i, source):
        return remote(cross.at[k, source], back.at[k, r], ts.at[k, i], tr.at[k, i], (source, c))

    def product(k):
        twice = dot(jnp.concatenate([phi[...], plo[...]], axis=0), xhi[k])
        value = twice[0:slots] + twice[slots : 2 * slots] + dot(phi[...], xlo[k])
        cross[k] = value.reshape(NROW, CAP, CHUNK)
        for i in range(7):
            returned(k, i, row_dev(i)).start()
        back[k, r] = cross[k, r]

    def scatter(k):
        high, low = split(jnp.concatenate([back[k].reshape(slots, CHUNK), bsib[k].reshape(slots, CHUNK)], axis=0))
        value = dot(onehot[...].reshape(4 * group, 4 * slots), jnp.concatenate([high, low], axis=0))
        for i in range(8):
            mine[k, units[i]] += value[i * PAD : (i + 1) * PAD] + crecv[k, units[i]]

    def to_sibling(k):
        return remote(sib.at[k], crecv.at[k], cs.at[k], cr.at[k], sibling)

    def unit(k, depth, side):
        return mine.at[k, side * 4 + depth]

    def pass_on(k):
        return remote(back.at[k], bsib.at[k], bs.at[k], br.at[k], sibling)

    def around(k, i):
        source, device = [
            (unit(k, z2, 0), above),
            (unit(k, z2, 1), below),
            (unit(k, zp, 1), above),
            (unit(k, zm, 0), below),
            (unit(k, zp, 0), above),
            (unit(k, zm, 1), below),
        ][i]
        return remote(source, zrecv.at[k, i], zs.at[k, i], zr.at[k, i], device)

    quarter = CHUNK // 2
    same, other = yl * 4, (1 - yl) * 4

    def far_around(k, i):
        source, target, device = [
            (unit(k, zp, 1 - yl), zrecv.at[k, 0], above),
            (unit(k, zm, 1 - yl), zrecv.at[k, 1], below),
            (unit(k, z2, yl).at[:, 0:quarter], zrecv.at[k, 2, :, 0:quarter], above),
            (unit(k, z2, yl).at[:, quarter:CHUNK], zrecv.at[k, 3, :, quarter:CHUNK], below),
            (unit(k, zp, yl), zrecv.at[k, 4], above),
            (unit(k, zm, yl), zrecv.at[k, 5], below),
        ][i]
        return remote(source, target, zs.at[k, i], zr.at[k, i], device)

    def aside(k, i):
        return remote(unit(k, z if i else z2, 1 - yl), yrecv.at[k, i], ys.at[k, i], yr.at[k, i], beside)

    def exchange(k):
        return remote(esend.at[k], erecv.at[k], es.at[k], er.at[k], sibling)

    def solve(k, half_index, value):
        columns = pl.ds(pl.multiple_of(half_index * width + k * CHUNK, CHUNK), CHUNK)
        out[:, columns] = (drv[:, columns] + value) / den[:, columns]

    def late(k):
        both(k, 1)
        to_sibling(k).start()

    product(0)
    product(1)
    late(0)
    load_drv.wait()
    load_den.wait()
    block = rows // 2
    final = yl * 4 + z

    @pl.loop(0, chunks + 4)
    def _(t):
        @pl.when(t < chunks)
        def _():
            for i in range(7):
                remote(
                    cross.at[t, r], back.at[t, row_src(i)], ts.at[t, i], tr.at[t, i], (row_src(i), c)
                ).wait_recv()
            pass_on(t).start()

            @pl.when(t + 2 < chunks)
            def _():
                product(t + 2)

        @pl.when(t + 1 < chunks)
        def _():
            late(t + 1)

        @pl.when((t >= FAR + 1) & (t < chunks + 1))
        def _():
            k = t - 1
            aside(k, 0).wait_recv()
            mine[k, same + z2] += yrecv[k, 0]
            far_around(k, 2).start()
            far_around(k, 3).start()

        @pl.when(t < chunks)
        def _():
            to_sibling(t).wait_recv()
            pass_on(t).wait_recv()
            scatter(t)

        @pl.when(t < FAR)
        def _():
            for i in range(4):
                around(t, i).start()

        @pl.when((t >= FAR) & (t < chunks))
        def _():
            aside(t, 0).start()
            far_around(t, 0).start()
            far_around(t, 1).start()

        @pl.when((t >= FAR + 1) & (t < chunks + 1))
        def _():
            k = t - 1
            far_around(k, 0).wait_recv()
            far_around(k, 1).wait_recv()
            mine[k, other + z] += zrecv[k, 0] + zrecv[k, 1]
            aside(k, 1).start()
            far_around(k, 2).wait_recv()
            mine[k, same + zp, :, 0:quarter] += zrecv[k, 2, :, 0:quarter]
            far_around(k, 4).start()
            far_around(k, 3).wait_recv()
            mine[k, same + zm, :, quarter:CHUNK] += zrecv[k, 3, :, quarter:CHUNK]
            far_around(k, 5).start()

        @pl.when((t >= 1) & (t < FAR + 1))
        def _():
            k = t - 1
            around(k, 0).wait_recv()
            mine[k, zp] += zrecv[k, 0]
            around(k, 4).start()
            around(k, 1).wait_recv()
            mine[k, 4 + zm] += zrecv[k, 1]
            around(k, 5).start()

        @pl.when((t >= 2) & (t < FAR + 2))
        def _():
            k = t - 2
            for i in range(2, 6):
                around(k, i).wait_recv()
            mine[k, z] += zrecv[k, 3] + zrecv[k, 4]
            mine[k, 4 + z] += zrecv[k, 2] + zrecv[k, 5]
            aside(k, 1).start()

        @pl.when((t >= 3) & (t < chunks + 3))
        def _():
            k = t - 3

            @pl.when(k >= FAR)
            def _():
                far_around(k, 4).wait_recv()
                far_around(k, 5).wait_recv()
                mine[k, final] += zrecv[k, 4] + zrecv[k, 5]

            aside(k, 1).wait_recv()
            mine[k, final] += yrecv[k, 1]
            low = mine[k, final, 0:block, :]
            high = mine[k, final, block:rows, :]
            esend[k] = jnp.where(core == 0, high, low)
            exchange(k).start()
            solve(k, core, jnp.where(core == 0, low, high))

        @pl.when(t >= 4)
        def _():
            k = t - 4
            exchange(k).wait_recv()
            solve(k, 1 - core, erecv[k])

    for copy in sends + [g6, g7, g8, g9, tcopy] + mcopies:
        copy.wait_send()

    @pl.loop(0, chunks)
    def _(k):
        for i in range(7):
            returned(k, i, row_dev(i)).wait_send()
        to_sibling(k).wait_send()
        aside(k, 1).wait_send()
        pass_on(k).wait_send()
        exchange(k).wait_send()

    @pl.loop(0, FAR)
    def _(k):
        for i in range(6):
            around(k, i).wait_send()

    @pl.loop(FAR, chunks)
    def _(k):
        for i in range(6):
            far_around(k, i).wait_send()
        aside(k, 0).wait_send()


def tables(shard, channel_slot, channel_of, source_row, target_row, recoupling, meta, tgt):
    items = channel_of.shape[1]
    channel = channel_of[...]
    owner = jnp.zeros(channel.shape, jnp.int32)
    for i in range(NROW):
        owner = jnp.where(channel == i, channel_slot[i], owner)
    marks = jnp.where(lax.broadcasted_iota(jnp.int32, (NROW, items), 0) == owner, 1.0, 0.0)
    square = (items, items)
    down, along = lax.broadcasted_iota(jnp.int32, square, 0), lax.broadcasted_iota(jnp.int32, square, 1)
    before = dot(marks.astype(BF16), jnp.where(down < along, 1.0, 0.0).astype(BF16))
    slot = owner.astype(F32) * CAP + jnp.sum(marks * before, axis=0, keepdims=True)

    def padded(row):
        passed = row
        for i in range(1, NROW):
            passed = passed + jnp.where(row >= i * shard, PAD - shard, 0)
        return passed.astype(F32)

    def column(row):
        return jnp.sum(jnp.where(down == along, row, 0.0), axis=1, keepdims=True)

    target = target_row[...]
    slot_c, scale_c = column(slot), column(recoupling[...])
    source_c, hole_c = column(padded(source_row[...])), column(padded(target >> 1))
    odd_c = column((target & 1).astype(F32))
    lanes = along.astype(F32)
    for i in range(NROW):
        match = slot_c == lanes + i * CAP
        meta[i, 0:1, :] = jnp.sum(jnp.where(match, source_c + 1.0, 0.0), axis=0, keepdims=True) - 1.0
        meta[i, 1:2, :] = jnp.sum(jnp.where(match, scale_c, 0.0), axis=0, keepdims=True)
        meta[i, 2:8, :] = jnp.zeros((6, items), F32)
    slots = NROW * CAP
    match = slot_c == lax.broadcasted_iota(jnp.int32, (items, slots), 1).astype(F32)
    for i in range(2):
        hit = match & (odd_c == float(i))
        tgt[i : i + 1, :] = jnp.sum(jnp.where(hit, hole_c + 1.0, 0.0), axis=0, keepdims=True) - 1.0


def on_device(
    amplitude,
    ladder_coupling,
    crossed_coupling,
    channel_slot,
    channel_of,
    source_row,
    target_row,
    recoupling,
    driving,
    denominator,
):
    rows, width = amplitude.shape
    chunks = width // CHUNK
    slots = NROW * CAP
    group = 2 * PAD
    dma = pltpu.SemaphoreType.DMA
    vmem = pltpu.VMEM
    return pl.pallas_call(
        kernel,
        out_shape=jax.ShapeDtypeStruct((rows // 2, 2 * width), F32),
        in_specs=[pl.BlockSpec(memory_space=pltpu.SMEM)]
        + [pl.BlockSpec(memory_space=pltpu.VMEM)] * 4
        + [pl.BlockSpec(memory_space=pl.ANY)] * 5,
        out_specs=pl.BlockSpec(memory_space=pltpu.VMEM),
        scratch_shapes=[
            vmem((rows, width), F32),
            vmem((NROW, PAD, width), F32),
            vmem((4, group, width), BF16),
            vmem((4, group, width), BF16),
            vmem((2, CHUNK, width), F32),
            vmem((2 * chunks, CHUNK, width), BF16),
            vmem((2 * chunks, CHUNK, width), BF16),
            vmem((2, width, CHUNK), F32),
            vmem((chunks, width, CHUNK), BF16),
            vmem((chunks, width, CHUNK), BF16),
            vmem((NROW, 8, 128), F32),
            vmem((NROW, 8, 128), F32),
            vmem((2, slots), F32),
            vmem((2, slots), F32),
            vmem((1, 2 * slots), F32),
            vmem((slots, 128), F32),
            vmem((slots, 128), F32),
            vmem((slots, width), F32),
            vmem((slots, width), BF16),
            vmem((slots, width), BF16),
            vmem((4, group, 4 * slots), BF16),
            vmem((chunks, NROW, CAP, CHUNK), F32),
            vmem((chunks, NROW, CAP, CHUNK), F32),
            vmem((chunks, NROW, CAP, CHUNK), F32),
            vmem((chunks, NROW, PAD, CHUNK), F32),
            vmem((chunks, NROW, PAD, CHUNK), F32),
            vmem((chunks, NROW, PAD, CHUNK), F32),
            vmem((chunks, 6, PAD, CHUNK), F32),
            vmem((chunks, 2, PAD, CHUNK), F32),
            vmem((chunks, rows // 2, CHUNK), F32),
            vmem((chunks, rows // 2, CHUNK), F32),
            vmem((rows // 2, 2 * width), F32),
            vmem((rows // 2, 2 * width), F32),
            dma((3,)),
            dma((4,)),
            dma((12,)),
            dma((12,)),
            dma((8,)),
            dma((8,)),
            dma((chunks, 7)),
            dma((chunks, 7)),
            dma((chunks,)),
            dma((chunks,)),
            dma((chunks,)),
            dma((chunks,)),
            dma((chunks, 6)),
            dma((chunks, 6)),
            dma((chunks, 2)),
            dma((chunks, 2)),
            dma((chunks,)),
            dma((chunks,)),
        ],
        compiler_params=pltpu.CompilerParams(
            collective_id=0, has_side_effects=True, vmem_limit_bytes=63 * 1024 * 1024
        ),
        cost_estimate=pl.CostEstimate(flops=24_000_000_000, bytes_accessed=22_000_000, transcendentals=0),
    )(
        channel_slot,
        channel_of.reshape(1, -1),
        source_row,
        target_row,
        recoupling,
        amplitude,
        ladder_coupling,
        crossed_coupling,
        driving,
        denominator,
    )


def solution(mesh):
    in_specs = (
        P("row", "col"),
        P("row", "col"),
        P("row", None, None),
        P(),
        P("col", "row", None),
        P("col", "row"),
        P("col", "row"),
        P("col", "row"),
        P("col", "row"),
        P("col", "row"),
    )
    out_specs = P("col", "row")
    return jax.shard_map(
        on_device, mesh=mesh, in_specs=in_specs, out_specs=out_specs, check_vma=False
    )
```
